256 devices in a mesh: row: 16 (over z, y_hi), col: 16 (over y_lo, x, core).
Axes of the slice: x: 4, y: 4 (y_hi: 2, y_lo: 2; y = y_hi * 2 + y_lo), z: 8, core: 2. Of those that a mesh axis runs over, the one named last changes fastest.
Arguments:
- object_field: float32 [2, 4096, 4096], P(None, 'row', 'col'), may hold values from -5 to 5
- probe: float32 [2, 256, 256], replicated, may hold values from -6 to 6
- amplitudes: float32 [16, 16, 4, 256, 256], P('row', 'col'), may hold values from 0 to 11, as said below
- positions: int32 [16, 16, 4, 2], P('row', 'col'), may hold values from 0 to 64
Outputs:
- object_next: float32 [2, 4096, 4096], P(None, 'row', 'col')
- probe_next: float32 [2, 256, 256], replicated
The draws below stay inside these ranges and needn't reach their ends.
Inputs may be any that keep to these rules, and one draw needn't show every extreme that they name: Positive amplitudes.
All inputs are finite; a program needn't handle non-finite values.
Results may differ from the reference program's by a relative error of at most 0.0003.
Values sent between devices are 32-bit elements; how exact they have to be, the bound alone decides.
A program may use at most 64 MiB of HBM per device.

```python
import math
import jax
import jax.numpy as jnp
from jax import lax

W = 256
TILE = 256
MARGIN = 32
FRAMES = 4
TILES_R = 16
TILES_C = 16


def draw_amplitudes(key, part):
    first = jax.random.fold_in(key, 0)
    row_frac = jnp.arange(TILES_R, dtype=jnp.float32) / max(TILES_R - 1, 1)
    col_frac = jnp.arange(TILES_C, dtype=jnp.float32) / max(TILES_C - 1, 1)
    spread = 0.5 * (row_frac[:, None] + col_frac[None, :])
    scaling = jnp.sqrt(1.0 + 2.0 * spread)[:, :, None, None, None]
    normal_draw = jax.random.normal(first, (TILES_R, TILES_C, FRAMES, W, W), jnp.float32)
    base = jnp.exp(0.5 * jnp.clip(normal_draw, -3.0, 3.0))
    factor = jnp.ones((TILES_R, TILES_C, FRAMES, 1, 1), jnp.float32)
    return (scaling * factor * base).astype(jnp.float32)


def place_ends(array, rng, smallest, top_value):
    longest = array.shape.index(max(array.shape))
    spots = []
    for shift in (0, 1):
        where = [jax.random.randint(jax.random.fold_in(rng, axis), (), 0, length) for axis, length in enumerate(array.shape)]
        where[longest] = (where[longest] + shift) % array.shape[longest]
        spots.append(tuple(where))
    return array.at[spots[0]].set(smallest).at[spots[1]].set(top_value)


def level_of(stream_key, extent, shards, smallest, largest):
    factor_of = 1.0
    for axis_at, blocks in shards:
        draws = jax.random.uniform(jax.random.fold_in(jax.random.fold_in(stream_key, 6), axis_at), (blocks,), jnp.float32, smallest / len(shards), largest / len(shards))
        factor_of = factor_of * jnp.repeat(jnp.exp(draws), extent[axis_at] // blocks).reshape((-1,) + (1,) * (len(extent) - 1 - axis_at))
    return factor_of


def scatter_about(own_key, shape, width, limit, cuts=(), held_as=jnp.bfloat16):
    values = width * jax.random.normal(own_key, shape, jnp.float32)
    if cuts:
        values = values * level_of(own_key, shape, cuts, -0.22, 0.18)
    return jnp.clip(values, -limit, limit).astype(held_as)


def setup_inputs(seed: int = 0) -> dict:
    streams_of = jax.random.split(jax.random.key(seed), 5)
    object_field = scatter_about(streams_of[0], (2, TILES_R * TILE, TILES_C * TILE), 0.7, 5.0, ((1, 16), (2, 16)), jnp.float32)
    probe = scatter_about(streams_of[1], (2, W, W), 1.0, 6.0, (), jnp.float32)
    amplitudes = draw_amplitudes(jax.random.fold_in(streams_of[4], 71), 0)
    positions = place_ends(jax.random.randint(streams_of[3], (TILES_R, TILES_C, FRAMES, 2), 0, TILE + 2 * MARGIN - W + 1), jax.random.fold_in(streams_of[3], 1), 0, TILE + 2 * MARGIN - W).astype(jnp.int32)
    return {"object_field": object_field, "probe": probe, "amplitudes": amplitudes, "positions": positions}


smoothing = 0.1
regular = 1.0
epsilon = 1e-06

def tables(length):
    indices = jnp.arange(length, dtype=jnp.int32)
    phases = (indices[:, None] * indices[None, :] % length).astype(jnp.float32) * (2.0 * math.pi / length)
    scaling = 1.0 / math.sqrt(length)
    cosine = jnp.cos(phases) * scaling
    sines = jnp.sin(phases) * scaling
    forward = jnp.concatenate([jnp.concatenate([cosine, sines], 1), jnp.concatenate([-sines, cosine], 1)], 0)
    inverse = jnp.concatenate([jnp.concatenate([cosine, -sines], 1), jnp.concatenate([sines, cosine], 1)], 0)
    return (forward, inverse)

def transform(wavefield, left_matrix, right_matrix):
    length = wavefield.shape[1]
    stacked = wavefield.reshape(2 * length, length)
    mixed = jnp.dot(left_matrix, stacked, precision=lax.Precision.HIGHEST)
    paired = jnp.concatenate([mixed[:length], mixed[length:]], axis=1)
    result = jnp.dot(paired, right_matrix, precision=lax.Precision.HIGHEST)
    return jnp.stack([result[:, :length], result[:, length:]])

def frame_terms(probe, window, amplitude, forward, inverse):
    exit_real = probe[0] * window[0] - probe[1] * window[1]
    exit_imag = probe[0] * window[1] + probe[1] * window[0]
    wave = jnp.stack([exit_real, exit_imag])
    far_field = transform(wave, forward, inverse)
    factor = amplitude / jnp.sqrt(far_field[0] * far_field[0] + far_field[1] * far_field[1] + smoothing)
    near_field = transform(far_field * factor[None], inverse, forward)
    difference = near_field - wave
    object_real = probe[0] * difference[0] + probe[1] * difference[1]
    object_imag = probe[0] * difference[1] - probe[1] * difference[0]
    probe_real = window[0] * difference[0] + window[1] * difference[1]
    probe_imag = window[0] * difference[1] - window[1] * difference[0]
    window_power = window[0] * window[0] + window[1] * window[1]
    return (jnp.stack([object_real, object_imag]), jnp.stack([probe_real, probe_imag, window_power]))

def reference(object_field, probe, amplitudes, positions):
    forward, inverse = tables(W)
    height = TILES_R * TILE
    breadth = TILES_C * TILE
    padded = jnp.pad(object_field, ((0, 0), (MARGIN, MARGIN), (MARGIN, MARGIN)))
    power_map = probe[0] * probe[0] + probe[1] * probe[1]
    frame_count = TILES_R * TILES_C * FRAMES
    measured = amplitudes.reshape(frame_count, W, W)
    offsets = positions.reshape(frame_count, 2).astype(jnp.int32)
    tile_flat = jnp.arange(frame_count, dtype=jnp.int32) // FRAMES
    tile_rows = tile_flat // TILES_C
    tile_cols = tile_flat % TILES_C

    def visit(carried, inputs):
        canvas, probe_acc = carried
        amplitude, offset, tile_row, tile_col = inputs
        row_start = (tile_row * TILE + offset[0]).astype(jnp.int32)
        col_start = (tile_col * TILE + offset[1]).astype(jnp.int32)
        anchor = jnp.zeros((), jnp.int32)
        window = lax.dynamic_slice(padded, (anchor, row_start, col_start), (2, W, W))
        object_term, probe_term = frame_terms(probe, window, amplitude, forward, inverse)
        update = jnp.concatenate([object_term, power_map[None]], 0)
        current = lax.dynamic_slice(canvas, (anchor, row_start, col_start), (3, W, W))
        canvas = lax.dynamic_update_slice(canvas, current + update, (anchor, row_start, col_start))
        return ((canvas, probe_acc + probe_term), None)
    canvas_start = jnp.zeros((3, height + 2 * MARGIN, breadth + 2 * MARGIN), jnp.float32)
    probe_start = jnp.zeros((3, W, W), jnp.float32)
    (canvas, probe_acc), _ = lax.scan(visit, (canvas_start, probe_start), (measured, offsets, tile_rows, tile_cols))
    interior = canvas[:, MARGIN:MARGIN + height, MARGIN:MARGIN + breadth]
    object_next = object_field + interior[0:2] / (interior[2] + regular)
    stepped = probe + probe_acc[0:2] / (probe_acc[2] + regular)
    target = jnp.sum(amplitudes * amplitudes) / frame_count
    probe_power = jnp.sum(stepped * stepped)
    probe_next = stepped * jnp.sqrt(target / (probe_power + epsilon))
    return (object_next, probe_next)
```

```python
import functools
import math

import jax
import jax.numpy as jnp
import numpy as np
from jax import lax
from jax.experimental import pallas as pl
from jax.experimental.pallas import tpu as pltpu
from jax.sharding import PartitionSpec as P

W = 256
HALF = W // 2
MARGIN = 32
FRAMES = 4
SIDE = W + 2 * MARGIN
LEAD = 2 * MARGIN

smoothing = 0.1
regular = 1.0
epsilon = 1e-06

MESH = pl.DeviceIdType.MESH
F32 = jnp.float32
BF16 = jnp.bfloat16

COMPASS = ((-1, 0), (1, 0), (0, -1), (0, 1), (-1, -1), (-1, 1), (1, -1), (1, 1))


def dft_tables():
    k = np.arange(HALF)
    j = np.arange(HALF)
    mats = []
    for parity in (0, 1):
        phase = (2 * k[:, None] + parity) * j[None, :] % W
        z = np.exp(-2j * np.pi * phase / W) / math.sqrt(W)
        mats.append(np.block([[z.real, -z.imag], [z.imag, z.real]]))
    mats += [m.T for m in mats]
    full = np.stack(mats)
    high = full.astype(BF16)
    low = (full - high.astype(np.float64)).astype(BF16)
    return np.stack([high, low], 1)


def sort_table():
    table = np.zeros((W, W), np.float32)
    k = np.arange(HALF)
    table[2 * k, k] = 1
    table[2 * k + 1, HALF + k] = 1
    return table.astype(BF16)


def split(x):
    high = x.astype(BF16)
    return high, (x - high.astype(F32)).astype(BF16)


def lanes(rows=8):
    return lax.broadcasted_iota(jnp.int32, (rows, 128), 1)


def greet(partners):
    barrier = pltpu.get_barrier_semaphore()
    for partner in partners:
        pl.semaphore_signal(barrier, inc=1, device_id=partner, device_id_type=MESH)
    pl.semaphore_wait(barrier, len(partners))


def neighbours(r, c, rows, cols):
    return [(lax.rem(r + dr + rows, rows), lax.rem(c + dc + cols, cols)) for dr, dc in COMPASS]


def pack(blocks, shift):
    group = lanes() // 32
    out = None
    for q, block in enumerate(blocks):
        amount = (shift + 32 * q) % 128
        turned = pltpu.roll(block, amount, 1) if amount else block
        out = turned if out is None else jnp.where(group == q, turned, out)
    return out


def halo_kernel(rows, cols, obj, ext, strips, from_ns, from_we, from_corner, send_sem, recv_sem):
    r, c = lax.axis_index("row"), lax.axis_index("col")
    around = neighbours(r, c, rows, cols)
    barrier = pltpu.get_barrier_semaphore()
    for partner in around:
        pl.semaphore_signal(barrier, inc=1, device_id=partner, device_id_type=MESH)
    for p in range(2):
        for j in range(8):
            left = [obj[p, pl.ds(32 * j + 8 * q, 8), 0:128] for q in range(4)]
            right = [obj[p, pl.ds(32 * j + 8 * q, 8), 128:256] for q in range(4)]
            strips[0, p, pl.ds(8 * j, 8), :] = pack(left, 0)
            strips[1, p, pl.ds(8 * j, 8), :] = pack(right, 32)
    pl.semaphore_wait(barrier, len(around))
    moves = (
        (obj.at[:, 0:32, :], from_ns.at[1]),
        (obj.at[:, W - 32 : W, :], from_ns.at[0]),
        (strips.at[0], from_we.at[1]),
        (strips.at[1], from_we.at[0]),
        (strips.at[0, :, 0:8, :], from_corner.at[3]),
        (strips.at[1, :, 0:8, :], from_corner.at[2]),
        (strips.at[0, :, 56:64, :], from_corner.at[1]),
        (strips.at[1, :, 56:64, :], from_corner.at[0]),
    )
    copies = []
    for i, (src, dst) in enumerate(moves):
        copies.append(
            pltpu.make_async_remote_copy(
                src_ref=src,
                dst_ref=dst,
                send_sem=send_sem.at[i],
                recv_sem=recv_sem.at[i],
                device_id=around[i],
                device_id_type=MESH,
            )
        )
    for i in (4, 5, 6, 7, 0, 1, 2, 3):
        copies[i].start()
    for copy in copies:
        copy.wait()
    lane = lanes()
    first = lane < 32
    second = lane < 64
    zero = jnp.zeros((8, 128), F32)
    has_n, has_s = r > 0, r < rows - 1
    has_w, has_e = c > 0, c < cols - 1

    def strip(ref, at, q, target, keep):
        amount = (target - 32 * q) % 128
        block = ref[at]
        block = pltpu.roll(block, amount, 1) if amount else block
        return jnp.where(keep, block, zero)

    def place(p, row, centre, west, east):
        t0, t1 = pltpu.roll(centre[0], 32, 1), pltpu.roll(centre[1], 32, 1)
        ext[p, 0, pl.ds(row, 8), :] = jnp.where(first, west, t0)
        ext[p, 1, pl.ds(row, 8), :] = jnp.where(first, t0, t1)
        ext[p, 2, pl.ds(row, 8), :] = jnp.where(first, t1, jnp.where(second, east, zero))

    for p in range(2):
        for k in range(4):
            for side, (keep_v, base) in enumerate(((has_n, 0), (has_s, MARGIN + W))):
                block = from_ns[side, p, pl.ds(8 * k, 8), :]
                block = jnp.where(keep_v, block, jnp.zeros_like(block))
                west = strip(from_corner, (2 * side, p, slice(0, 8)), k, 0, has_w & keep_v)
                east = strip(from_corner, (2 * side + 1, p, slice(0, 8)), k, 32, has_e & keep_v)
                place(p, base + 8 * k, (block[:, :128], block[:, 128:]), west, east)
        for j in range(8):
            for q in range(4):
                at = 32 * j + 8 * q
                block = obj[p, pl.ds(at, 8), :]
                west = strip(from_we, (0, p, pl.ds(8 * j, 8)), q, 0, has_w)
                east = strip(from_we, (1, p, pl.ds(8 * j, 8)), q, 32, has_e)
                place(p, MARGIN + at, (block[:, :128], block[:, 128:]), west, east)


def triple(left, right):
    a = jnp.concatenate([left[0], left[0], left[1]], axis=1)
    b = jnp.concatenate([right[0], right[1], right[0]], axis=0)
    return jnp.dot(a, b, preferred_element_type=F32)


STEP = 16


def frames_kernel(
    pos,
    ext,
    probe,
    amps_hbm,
    table,
    sort,
    canvas,
    acc,
    amp_sum,
    amps,
    spread,
    wave,
    win,
    sorted_amp,
    half,
    mid,
    out_mid,
    amp_sem,
):
    loads = []
    for f in range(FRAMES):
        for t in range(2):
            loads.append(
                pltpu.make_async_copy(
                    amps_hbm.at[f, :, 128 * t : 128 * t + 128], amps.at[f, t], amp_sem.at[2 * f + t]
                )
            )
            loads[-1].start()
    lane = lanes(STEP)
    zero = jnp.zeros((STEP, 128), F32)

    def clear(i, _):
        for f in range(FRAMES):
            for p in range(3):
                blank = jnp.zeros((16, 128), F32)
                for t in range(3):
                    spread[f, p, t, pl.ds(16 * i, 16), :] = blank
                    spread[f, p, t, pl.ds(LEAD + W + 16 * i, 16), :] = blank
        return 0

    lax.fori_loop(0, LEAD // 16, clear, 0)

    def clear_acc(i, _):
        for p in range(3):
            acc[p, pl.ds(32 * i, 32), :] = jnp.zeros((32, W), F32)
        return 0

    lax.fori_loop(0, W // 32, clear_acc, 0)

    sums = jnp.zeros((8, 128), F32)
    for f in range(FRAMES):
        loads[2 * f].wait()
        loads[2 * f + 1].wait()
        parts = []
        for parity in (0, 1):
            a = jnp.concatenate([amps[f, t, pl.ds(parity, HALF, stride=2), :] for t in range(2)], axis=1)
            squares = a * a
            sums = sums + (squares[:, :128] + squares[:, 128:]).reshape(16, 8, 128).sum(axis=0)
            high = a.astype(BF16)
            rest = a - high.astype(F32)
            middle = rest.astype(BF16)
            low = (rest - middle.astype(F32)).astype(BF16)
            parts.append(jnp.concatenate([high, middle, low], axis=1))
        both = jnp.concatenate(parts, axis=0)
        sorter = sort[...]
        sorted_amp[f] = jnp.dot(
            both, jnp.concatenate([sorter, sorter, sorter], axis=0), preferred_element_type=F32
        )
    amp_sum[...] = sums

    def visit(f, _):
        a = pos[2 * f]
        b = pos[2 * f + 1]
        back = lax.rem(128 - b, 128)
        keep = lane < 128 - b
        behind = lane >= b

        def gather(p, row):
            tiles = [ext[p, t, pl.ds(a + row, STEP), :] for t in range(3)]
            turned = [pltpu.roll(t, back, 1) for t in tiles]
            return jnp.concatenate(
                [jnp.where(keep, turned[0], turned[1]), jnp.where(keep, turned[1], turned[2])], axis=1
            )

        def scatter(p, row, value):
            v0, v1 = pltpu.roll(value[:, :128], b, 1), pltpu.roll(value[:, 128:], b, 1)
            at = pl.ds(LEAD + row, STEP)
            spread[f, p, 0, at, :] = jnp.where(behind, v0, zero)
            spread[f, p, 1, at, :] = jnp.where(behind, v1, v0)
            spread[f, p, 2, at, :] = jnp.where(behind, zero, v1)

        def first_step(i, _):
            at = [pl.multiple_of(STEP * i, STEP), pl.multiple_of(HALF + STEP * i, STEP)]
            waves = []
            for row in at:
                here = pl.ds(row, STEP)
                wr, wi = gather(0, row), gather(1, row)
                pr, pi = probe[0, here, :], probe[1, here, :]
                win[0, here, :] = wr
                win[1, here, :] = wi
                acc[2, here, :] += wr * wr + wi * wi
                er, ei = pr * wr - pi * wi, pr * wi + pi * wr
                wave[0, here, :] = er
                wave[1, here, :] = ei
                scatter(2, row, pr * pr + pi * pi)
                waves.append((er, ei))
            for part in range(2):
                top, low = waves[0][part], waves[1][part]
                for side, value in enumerate((top + low, top - low)):
                    h, l = split(value)
                    half[side, 0, pl.ds(HALF * part + at[0], STEP), :] = h
                    half[side, 1, pl.ds(HALF * part + at[0], STEP), :] = l
            return 0

        lax.fori_loop(0, HALF // STEP, first_step, 0)
        for side in range(2):
            mid[side] = triple((table[side, 0], table[side, 1]), (half[side, 0], half[side, 1]))

        def second_step(i, _):
            row = pl.multiple_of(STEP * i, STEP)
            for parity in range(2):
                zr = mid[parity, pl.ds(row, STEP), :]
                zi = mid[parity, pl.ds(HALF + row, STEP), :]
                here = pl.ds(HALF * parity + row, STEP)
                plus = jnp.concatenate([zr[:, :128] + zr[:, 128:], zi[:, :128] + zi[:, 128:]], axis=1)
                less = jnp.concatenate([zr[:, :128] - zr[:, 128:], zi[:, :128] - zi[:, 128:]], axis=1)
                for side, value in enumerate((plus, less)):
                    h, l = split(value)
                    half[side, 0, here, :] = h
                    half[side, 1, here, :] = l
            return 0

        lax.fori_loop(0, HALF // STEP, second_step, 0)
        for side in range(2):
            mid[side] = triple((half[side, 0], half[side, 1]), (table[2 + side, 0], table[2 + side, 1]))

        def third_step(i, _):
            here = pl.ds(pl.multiple_of(STEP * i, STEP), STEP)
            amp = sorted_amp[f, here, :]
            for side in range(2):
                z = mid[side, here, :]
                zr, zi = z[:, :128], z[:, 128:]
                factor = amp[:, 128 * side : 128 * side + 128] / jnp.sqrt(zr * zr + zi * zi + smoothing)
                h, l = split(jnp.concatenate([zr * factor, zi * factor], axis=1))
                half[side, 0, here, :] = h
                half[side, 1, here, :] = l
            return 0

        lax.fori_loop(0, W // STEP, third_step, 0)
        for side in range(2):
            out_mid[side] = triple((half[side, 0], half[side, 1]), (table[side, 0], table[side, 1]))

        def fourth_step(i, _):
            row = pl.multiple_of(STEP * i, STEP)
            for parity in range(2):
                here = pl.ds(HALF * parity + row, STEP)
                even, odd = out_mid[0, here, :], out_mid[1, here, :]
                plus, less = even + odd, even - odd
                for part in range(2):
                    value = jnp.concatenate(
                        [plus[:, 128 * part : 128 * part + 128], less[:, 128 * part : 128 * part + 128]], axis=1
                    )
                    h, l = split(value)
                    half[parity, 0, pl.ds(HALF * part + row, STEP), :] = h
                    half[parity, 1, pl.ds(HALF * part + row, STEP), :] = l
            return 0

        lax.fori_loop(0, HALF // STEP, fourth_step, 0)
        for side in range(2):
            mid[side] = triple((table[2 + side, 0], table[2 + side, 1]), (half[side, 0], half[side, 1]))

        def fifth_step(i, _):
            row = pl.multiple_of(STEP * i, STEP)
            er, orr = mid[0, pl.ds(row, STEP), :], mid[1, pl.ds(row, STEP), :]
            ei, oi = mid[0, pl.ds(HALF + row, STEP), :], mid[1, pl.ds(HALF + row, STEP), :]
            for sign, base in ((1, 0), (-1, HALF)):
                at = pl.multiple_of(base + row, STEP)
                here = pl.ds(at, STEP)
                nr, ni = (er + orr, ei + oi) if sign > 0 else (er - orr, ei - oi)
                dr, di = nr - wave[0, here, :], ni - wave[1, here, :]
                pr, pi = probe[0, here, :], probe[1, here, :]
                wr, wi = win[0, here, :], win[1, here, :]
                scatter(0, at, pr * dr + pi * di)
                scatter(1, at, pr * di - pi * dr)
                acc[0, here, :] += wr * dr + wi * di
                acc[1, here, :] += wr * di - wi * dr
            return 0

        lax.fori_loop(0, HALF // STEP, fifth_step, 0)
        return 0

    lax.fori_loop(0, FRAMES, visit, 0)

    def gather_canvas(i, _):
        row = pl.multiple_of(16 * i, 16)
        for p in range(3):
            for t in range(3):
                total = spread[0, p, t, pl.ds(LEAD - pos[0] + row, 16), :]
                for f in range(1, FRAMES):
                    total = total + spread[f, p, t, pl.ds(LEAD - pos[2 * f] + row, 16), :]
                canvas[p, t, pl.ds(row, 16), :] = total
        return 0

    lax.fori_loop(0, SIDE // 16, gather_canvas, 0)


def reduce_kernel(
    rows,
    cols,
    canvas,
    acc,
    amp,
    obj,
    probe,
    out_obj,
    out_probe,
    strips,
    bands,
    from_ns,
    from_we,
    from_corner,
    got0,
    part0,
    got1,
    part1,
    got2,
    part2,
    got3,
    gathered,
    amp0,
    amp1,
    amp2,
    amp3,
    send_edge,
    recv_edge,
    send_sem,
    recv_sem,
    send_amp,
    recv_amp,
    send_out,
    recv_out,
):
    r, c = lax.axis_index("row"), lax.axis_index("col")
    core, x, y_lo = lax.rem(c, 2), lax.rem(c // 2, 4), c // 8
    y_hi, z = lax.rem(r, 2), r // 2
    y = 2 * y_hi + y_lo

    def place(core_, x_, y_, z_):
        return (2 * z_ + y_ // 2, (lax.rem(y_, 2) * 4 + x_) * 2 + core_)

    around = neighbours(r, c, rows, cols)
    pair = place(1 - core, x, y, z)
    along_x = [place(core, lax.rem(x + d, 4), y, z) for d in range(1, 4)]
    along_y = [place(core, x, lax.rem(y + d, 4), z) for d in range(1, 4)]
    along_z = [place(core, x, y, lax.rem(z + d, 8)) for d in range(1, 8)]
    everyone = around + [pair] + along_x + along_y + along_z
    barrier = pltpu.get_barrier_semaphore()
    for partner in everyone:
        pl.semaphore_signal(barrier, inc=1, device_id=partner, device_id_type=MESH)

    lane = lanes()
    first = lane < 32
    zero = jnp.zeros((8, 128), F32)
    for p in range(3):
        for j in range(10):
            left = [canvas[p, 0, pl.ds(32 * j + 8 * q, 8), :] for q in range(4)]
            right = [canvas[p, 2, pl.ds(32 * j + 8 * q, 8), :] for q in range(4)]
            strips[0, p, pl.ds(8 * j, 8), :] = pack(left, 0)
            strips[1, p, pl.ds(8 * j, 8), :] = pack(right, 96)
        for side, base in enumerate((0, MARGIN + W)):
            for k in range(4):
                t = [pltpu.roll(canvas[p, i, pl.ds(base + 8 * k, 8), :], 96, 1) for i in range(3)]
                bands[side, p, pl.ds(8 * k, 8), 0:128] = jnp.where(lane < 96, t[0], t[1])
                bands[side, p, pl.ds(8 * k, 8), 128:256] = jnp.where(lane < 96, t[1], t[2])
    amp0[core] = amp[...]
    pl.semaphore_wait(barrier, len(everyone))

    def send(src, dst, sends, recvs, device):
        copy = pltpu.make_async_remote_copy(
            src_ref=src, dst_ref=dst, send_sem=sends, recv_sem=recvs, device_id=device, device_id_type=MESH
        )
        copy.start()
        return copy

    other = pl.ds(pl.multiple_of((1 - core) * HALF, HALF), HALF)
    mine = pl.ds(pl.multiple_of(core * HALF, HALF), HALF)
    c0 = send(acc.at[:, other, :], got0, send_sem.at[0], recv_sem.at[0], pair)
    a0 = send(amp0.at[core], amp0.at[core], send_amp.at[0], recv_amp.at[core], pair)
    moves = (
        (bands.at[0], from_ns.at[1]),
        (bands.at[1], from_ns.at[0]),
        (strips.at[0, :, 8:72, :], from_we.at[1]),
        (strips.at[1, :, 8:72, :], from_we.at[0]),
        (strips.at[0, :, 0:8, :], from_corner.at[3]),
        (strips.at[1, :, 0:8, :], from_corner.at[2]),
        (strips.at[0, :, 72:80, :], from_corner.at[1]),
        (strips.at[1, :, 72:80, :], from_corner.at[0]),
    )
    edges = [
        send(src, dst, send_edge.at[i], recv_edge.at[i], around[i]) for i, (src, dst) in enumerate(moves)
    ]

    def arrive(dst, recvs):
        pltpu.make_async_remote_copy(
            src_ref=dst, dst_ref=dst, send_sem=recvs, recv_sem=recvs, device_id=pair, device_id_type=MESH
        ).wait_recv()

    c0.wait_recv()
    for p in range(3):
        part0[p] = acc[p, mine, :] + got0[p]
    c1 = []
    for d in range(1, 4):
        to = lax.rem(x + d, 4)
        src = part0.at[:, pl.ds(pl.multiple_of(32 * to, 32), 32), :]
        c1.append(send(src, got1.at[d - 1], send_sem.at[d], recv_sem.at[d], along_x[d - 1]))
    arrive(amp0.at[1 - core], recv_amp.at[1 - core])
    amp1[x] = amp0[0] + amp0[1]
    a1 = [
        send(amp1.at[x], amp1.at[x], send_amp.at[d], recv_amp.at[2 + x], along_x[d - 1]) for d in range(1, 4)
    ]

    for e in edges:
        e.wait_recv()
    has_n, has_s = r > 0, r < rows - 1
    has_w, has_e = c > 0, c < cols - 1

    def strip(ref, at, q, target, keep):
        amount = (target - 32 * q) % 128
        block = ref[at]
        block = pltpu.roll(block, amount, 1) if amount else block
        return jnp.where(keep, block, zero)

    for j in range(8):
        for q in range(4):
            at = 32 * j + 8 * q
            totals = []
            for p in range(3):
                t = [pltpu.roll(canvas[p, i, pl.ds(MARGIN + at, 8), :], 96, 1) for i in range(3)]
                left = jnp.where(lane < 96, t[0], t[1])
                right = jnp.where(lane < 96, t[1], t[2])
                if j in (0, 7):
                    side = 0 if j == 0 else 1
                    keep_v = has_n if j == 0 else has_s
                    band = from_ns[side, p, pl.ds(8 * q, 8), :]
                    left = left + jnp.where(keep_v, band[:, :128], zero)
                    right = right + jnp.where(keep_v, band[:, 128:], zero)
                    west = strip(from_corner, (2 * side, p, slice(0, 8)), q, 0, has_w & keep_v)
                    east = strip(from_corner, (2 * side + 1, p, slice(0, 8)), q, 96, has_e & keep_v)
                    left = left + jnp.where(first, west, zero)
                    right = right + jnp.where(lane >= 96, east, zero)
                west = strip(from_we, (0, p, pl.ds(8 * j, 8)), q, 0, has_w)
                east = strip(from_we, (1, p, pl.ds(8 * j, 8)), q, 96, has_e)
                left = left + jnp.where(first, west, zero)
                right = right + jnp.where(lane >= 96, east, zero)
                totals.append((left, right))
            for s in range(2):
                scale = 1.0 / (totals[2][s] + regular)
                for p in range(2):
                    here = (p, pl.ds(at, 8), slice(128 * s, 128 * s + 128))
                    out_obj[here] = obj[here] + totals[p][s] * scale

    for d in range(1, 4):
        arrive(got1.at[d - 1], recv_sem.at[d])
    own = pl.ds(pl.multiple_of(32 * x, 32), 32)
    part1[...] = part0[:, own, :] + got1[0] + got1[1] + got1[2]
    c2 = []
    for d in range(1, 4):
        to = lax.rem(y + d, 4)
        src = part1.at[:, pl.ds(pl.multiple_of(8 * to, 8), 8), :]
        c2.append(send(src, got2.at[d - 1], send_sem.at[3 + d], recv_sem.at[3 + d], along_y[d - 1]))
    for d in range(1, 4):
        arrive(amp1.at[lax.rem(x + d, 4)], recv_amp.at[2 + lax.rem(x + d, 4)])
    amp2[y] = amp1[0] + amp1[1] + amp1[2] + amp1[3]
    a2 = [
        send(amp2.at[y], amp2.at[y], send_amp.at[3 + d], recv_amp.at[6 + y], along_y[d - 1]) for d in range(1, 4)
    ]
    for d in range(1, 4):
        arrive(got2.at[d - 1], recv_sem.at[3 + d])
    own = pl.ds(pl.multiple_of(8 * y, 8), 8)
    part2[...] = part1[:, own, :] + got2[0] + got2[1] + got2[2]

    base = lax.rem(x + y + 2 * core, 4)
    owners = [base, base + 4]
    for t in range(2):
        for d in range(8):
            here = lax.rem(owners[t] + d, 8)

            @pl.when(z == here)
            def _(t=t, d=d):
                if d == 0:
                    got3[0] = part2[:, :, 128 * t : 128 * t + 128]
                else:
                    send(
                        part2.at[:, :, 128 * t : 128 * t + 128],
                        got3.at[d],
                        send_sem.at[7 + t],
                        recv_sem.at[7 + d],
                        place(core, x, y, owners[t]),
                    )

    for d in range(1, 4):
        arrive(amp2.at[lax.rem(y + d, 4)], recv_amp.at[6 + lax.rem(y + d, 4)])
    amp3[z] = amp2[0] + amp2[1] + amp2[2] + amp2[3]
    a3 = [
        send(amp3.at[z], amp3.at[z], send_amp.at[6 + d], recv_amp.at[10 + z], along_z[d - 1]) for d in range(1, 8)
    ]
    block = pl.ds(pl.multiple_of(HALF * core + 32 * x + 8 * y, 8), 8)
    for t in range(2):
        cut = slice(128 * t, 128 * t + 128)

        @pl.when(z == owners[t])
        def _(t=t, cut=cut):
            for d in range(1, 8):
                arrive(got3.at[d], recv_sem.at[7 + d])
            total = got3[0]
            for d in range(1, 8):
                total = total + got3[d]
            scale = 1.0 / (total[2] + regular)
            for p in range(2):
                gathered[p, block, cut] = probe[p, block, cut] + total[p] * scale
            for d in range(1, 8):
                send(
                    gathered.at[:, block, cut],
                    gathered.at[:, block, cut],
                    send_out.at[d - 1],
                    recv_out.at[t],
                    along_z[d - 1],
                )

    for t in range(2):
        cut = slice(128 * t, 128 * t + 128)

        @pl.when(z != owners[t])
        def _(t=t, cut=cut):
            arrive(gathered.at[:, block, cut], recv_out.at[t])

    g1 = [
        send(gathered.at[:, block, :], gathered.at[:, block, :], send_out.at[6 + d], recv_out.at[1 + d], along_y[d - 1])
        for d in range(1, 4)
    ]
    for d in range(1, 4):
        from_y = lax.rem(y + 4 - d, 4)
        at = pl.ds(pl.multiple_of(HALF * core + 32 * x + 8 * from_y, 8), 8)
        arrive(gathered.at[:, at, :], recv_out.at[1 + d])
    block = pl.ds(pl.multiple_of(HALF * core + 32 * x, 32), 32)
    g2 = [
        send(gathered.at[:, block, :], gathered.at[:, block, :], send_out.at[9 + d], recv_out.at[4 + d], along_x[d - 1])
        for d in range(1, 4)
    ]
    for d in range(1, 4):
        from_x = lax.rem(x + 4 - d, 4)
        at = pl.ds(pl.multiple_of(HALF * core + 32 * from_x, 32), 32)
        arrive(gathered.at[:, at, :], recv_out.at[4 + d])
    g3 = send(gathered.at[:, mine, :], gathered.at[:, mine, :], send_out.at[13], recv_out.at[8], pair)
    for d in range(1, 8):
        arrive(amp3.at[lax.rem(z + d, 8)], recv_amp.at[10 + lax.rem(z + d, 8)])
    whole = amp3[0]
    for i in range(1, 8):
        whole = whole + amp3[i]
    target = jnp.sum(whole) * (1.0 / (FRAMES * rows * cols))
    arrive(gathered.at[:, other, :], recv_out.at[8])
    power = jnp.zeros((8, W), F32)
    for p in range(2):
        g = gathered[p]
        power = power + (g * g).reshape(32, 8, W).sum(axis=0)
    scale = jnp.sqrt(jnp.full((8, W), target, F32) / (jnp.sum(power) + epsilon))
    for p in range(2):
        out_probe[p] = gathered[p] * jnp.concatenate([scale] * 32, axis=0)

    for copy in [c0, a0, g3] + edges + c1 + a1 + c2 + a2 + a3 + g1 + g2:
        copy.wait_send()

    def left(src, sends):
        pltpu.make_async_remote_copy(
            src_ref=src, dst_ref=src, send_sem=sends, recv_sem=sends, device_id=pair, device_id_type=MESH
        ).wait_send()

    for t in range(2):
        cut = slice(128 * t, 128 * t + 128)

        @pl.when(z != owners[t])
        def _(t=t, cut=cut):
            left(part2.at[:, :, cut], send_sem.at[7 + t])

        @pl.when(z == owners[t])
        def _(t=t, cut=cut):
            for d in range(1, 8):
                left(part2.at[0:2, :, cut], send_out.at[d - 1])


def vmem(*shape, dtype=F32):
    return pltpu.VMEM(shape, dtype)


def per_device(rows, cols, object_field, probe, amplitudes, positions):
    in_vmem = pl.BlockSpec(memory_space=pltpu.VMEM)
    in_smem = pl.BlockSpec(memory_space=pltpu.SMEM)
    dma = pltpu.SemaphoreType.DMA
    ext = pl.pallas_call(
        functools.partial(halo_kernel, rows, cols),
        out_shape=jax.ShapeDtypeStruct((2, 3, SIDE, 128), F32),
        in_specs=[in_vmem],
        out_specs=in_vmem,
        scratch_shapes=[
            vmem(2, 2, 64, 128),
            vmem(2, 2, 32, W),
            vmem(2, 2, 64, 128),
            vmem(4, 2, 8, 128),
            dma((8,)),
            dma((8,)),
        ],
        compiler_params=pltpu.CompilerParams(collective_id=0, has_side_effects=True),
        name="halo",
    )(object_field)

    canvas, acc, amp = pl.pallas_call(
        frames_kernel,
        out_shape=(
            jax.ShapeDtypeStruct((3, 3, SIDE, 128), F32),
            jax.ShapeDtypeStruct((3, W, W), F32),
            jax.ShapeDtypeStruct((8, 128), F32),
        ),
        in_specs=[in_smem, in_vmem, in_vmem, pl.BlockSpec(memory_space=pl.ANY), in_vmem, in_vmem],
        out_specs=(in_vmem,) * 3,
        scratch_shapes=[
            vmem(FRAMES, 2, W, 128),
            vmem(FRAMES, 3, 3, LEAD + W + LEAD, 128),
            vmem(2, W, W),
            vmem(2, W, W),
            vmem(FRAMES, W, W),
            vmem(2, 2, W, W, dtype=BF16),
            vmem(2, W, W),
            vmem(2, W, W),
            dma((2 * FRAMES,)),
        ],
        compiler_params=pltpu.CompilerParams(vmem_limit_bytes=56 * 2**20),
        name="frames",
    )(
        positions.reshape(2 * FRAMES),
        ext,
        probe,
        amplitudes[0, 0],
        jnp.asarray(dft_tables()),
        jnp.asarray(sort_table()),
    )

    return pl.pallas_call(
        functools.partial(reduce_kernel, rows, cols),
        out_shape=(jax.ShapeDtypeStruct((2, W, W), F32),) * 2,
        in_specs=[in_vmem] * 5,
        out_specs=(in_vmem,) * 2,
        scratch_shapes=[
            vmem(2, 3, 80, 128),
            vmem(2, 3, 32, W),
            vmem(2, 3, 32, W),
            vmem(2, 3, 64, 128),
            vmem(4, 3, 8, 128),
            vmem(3, HALF, W),
            vmem(3, HALF, W),
            vmem(3, 3, 32, W),
            vmem(3, 32, W),
            vmem(3, 3, 8, W),
            vmem(3, 8, W),
            vmem(8, 3, 8, 128),
            vmem(2, W, W),
            vmem(2, 8, 128),
            vmem(4, 8, 128),
            vmem(4, 8, 128),
            vmem(8, 8, 128),
            dma((8,)),
            dma((8,)),
            dma((9,)),
            dma((15,)),
            dma((14,)),
            dma((18,)),
            dma((14,)),
            dma((9,)),
        ],
        compiler_params=pltpu.CompilerParams(
            collective_id=1, has_side_effects=True, vmem_limit_bytes=40 * 2**20
        ),
        name="reduce",
    )(canvas, acc, amp, object_field, probe)


def solution(mesh):
    return jax.shard_map(
        functools.partial(per_device, mesh.shape["row"], mesh.shape["col"]),
        mesh=mesh,
        in_specs=(
            P(None, "row", "col"),
            P(),
            P("row", "col", None, None, None),
            P("row", "col", None, None),
        ),
        out_specs=(P(None, "row", "col"), P()),
        check_vma=False,
    )
```

```python
import functools
import math

import jax
import jax.numpy as jnp
import numpy as np
from jax import lax
from jax.experimental import pallas as pl
from jax.experimental.pallas import tpu as pltpu
from jax.sharding import PartitionSpec as P

W = 256
HALF = W // 2
MARGIN = 32
FRAMES = 4
SIDE = W + 2 * MARGIN
LEAD = 2 * MARGIN

smoothing = 0.1
regular = 1.0
epsilon = 1e-06

MESH = pl.DeviceIdType.MESH
F32 = jnp.float32
BF16 = jnp.bfloat16

COMPASS = ((-1, 0), (1, 0), (0, -1), (0, 1), (-1, -1), (-1, 1), (1, -1), (1, 1))


def dft_tables():
    k = np.arange(HALF)
    j = np.arange(HALF)
    mats = []
    for parity in (0, 1):
        phase = (2 * k[:, None] + parity) * j[None, :] % W
        z = np.exp(-2j * np.pi * phase / W) / math.sqrt(W)
        mats.append(np.block([[z.real, -z.imag], [z.imag, z.real]]))
    mats += [m.T for m in mats]
    full = np.stack(mats)
    high = full.astype(BF16)
    low = (full - high.astype(np.float64)).astype(BF16)
    return np.stack([high, low], 1)


def sort_table():
    table = np.zeros((W, W), np.float32)
    k = np.arange(HALF)
    table[2 * k, k] = 1
    table[2 * k + 1, HALF + k] = 1
    return table.astype(BF16)


def split(x):
    high = x.astype(BF16)
    return high, (x - high.astype(F32)).astype(BF16)


def lanes(rows=8):
    return lax.broadcasted_iota(jnp.int32, (rows, 128), 1)


def neighbours(r, c, rows, cols):
    return [(lax.rem(r + dr + rows, rows), lax.rem(c + dc + cols, cols)) for dr, dc in COMPASS]


def pack(blocks, shift):
    group = lanes() // 32
    out = None
    for q, block in enumerate(blocks):
        amount = (shift + 32 * q) % 128
        turned = pltpu.roll(block, amount, 1) if amount else block
        out = turned if out is None else jnp.where(group == q, turned, out)
    return out


STEP = 16


def triple(left, right):
    a = jnp.concatenate([left[0], left[0], left[1]], axis=1)
    b = jnp.concatenate([right[0], right[1], right[0]], axis=0)
    return jnp.dot(a, b, preferred_element_type=F32)


def send(src, dst, sends, recvs, device):
    copy = pltpu.make_async_remote_copy(
        src_ref=src, dst_ref=dst, send_sem=sends, recv_sem=recvs, device_id=device, device_id_type=MESH
    )
    copy.start()
    return copy


def kernel(
    rows,
    cols,
    pos,
    obj_hbm,
    probe_hbm,
    amps_hbm,
    table_hbm,
    sort_hbm,
    out_obj,
    out_probe,
    obj,
    probe,
    amps,
    table,
    sort,
    halo_strips,
    halo_ns,
    halo_we,
    halo_corner,
    ext,
    spread,
    win,
    sorted_amp,
    half,
    mid,
    acc,
    power2,
    canvas,
    strips,
    bands,
    from_ns,
    from_we,
    from_corner,
    early0,
    early0_got,
    early1,
    early1_got,
    early2,
    got0,
    part0,
    got1,
    all2,
    gathered,
    load_sem,
    amp_sem,
    send_halo,
    recv_halo,
    send_edge,
    recv_edge,
    send_pair,
    recv_pair,
    send_e1,
    recv_e1,
    send_e2,
    recv_e2,
    send_m1,
    recv_m1,
    send_m2,
    recv_m2,
    send_ag,
    recv_ag,
    send_fw,
    recv_fw,
):
    loads = [
        pltpu.make_async_copy(src, dst, load_sem.at[i])
        for i, (src, dst) in enumerate(((obj_hbm, obj), (probe_hbm, probe), (sort_hbm, sort), (table_hbm, table)))
    ]
    loads[0].start()
    amp_loads = []
    for f in range(FRAMES):
        for t in range(2):
            amp_loads.append(
                pltpu.make_async_copy(
                    amps_hbm.at[0, 0, f, :, 128 * t : 128 * t + 128], amps.at[f, t], amp_sem.at[2 * f + t]
                )
            )

    r, c = lax.axis_index("row"), lax.axis_index("col")
    core, x, y_lo = lax.rem(c, 2), lax.rem(c // 2, 4), c // 8
    y_hi, z = lax.rem(r, 2), r // 2
    y = 2 * y_hi + y_lo

    def place(core_, x_, y_, z_):
        return (2 * z_ + y_ // 2, (lax.rem(y_, 2) * 4 + x_) * 2 + core_)

    around = neighbours(r, c, rows, cols)
    pair = place(1 - core, x, y, z)
    steps_xy = [(2, 2), (1, 2), (3, 2), (2, 1), (2, 3), (1, 1), (1, 3), (3, 1), (3, 3), (2, 0), (0, 2), (1, 0), (3, 0), (0, 1), (0, 3)]
    on_plane = [(lax.rem(x + dx, 4), lax.rem(y + dy, 4)) for dx, dy in steps_xy]
    behind_plane = [(lax.rem(x + 4 - dx, 4), lax.rem(y + 4 - dy, 4)) for dx, dy in steps_xy]
    plane = [place(core, x_, y_, z) for x_, y_ in on_plane]
    steps_z = [4, 3, 5, 2, 6, 1, 7]
    column = [place(core, x, y, lax.rem(z + d, 8)) for d in steps_z]
    everyone = around + [pair] + plane + column
    barrier = pltpu.get_barrier_semaphore()
    for partner in everyone:
        pl.semaphore_signal(barrier, inc=1, device_id=partner, device_id_type=MESH)
    loads[1].start()
    loads[2].start()
    for load in amp_loads:
        load.start()
    loads[3].start()

    loads[0].wait()
    for p in range(2):
        for j in range(8):
            left = [obj[p, pl.ds(32 * j + 8 * q, 8), 0:128] for q in range(4)]
            right = [obj[p, pl.ds(32 * j + 8 * q, 8), 128:256] for q in range(4)]
            halo_strips[0, p, pl.ds(8 * j, 8), :] = pack(left, 0)
            halo_strips[1, p, pl.ds(8 * j, 8), :] = pack(right, 32)
    pl.semaphore_wait(barrier, len(everyone))
    moves = (
        (obj.at[:, 0:32, :], halo_ns.at[1]),
        (obj.at[:, W - 32 : W, :], halo_ns.at[0]),
        (halo_strips.at[0], halo_we.at[1]),
        (halo_strips.at[1], halo_we.at[0]),
        (halo_strips.at[0, :, 0:8, :], halo_corner.at[3]),
        (halo_strips.at[1, :, 0:8, :], halo_corner.at[2]),
        (halo_strips.at[0, :, 56:64, :], halo_corner.at[1]),
        (halo_strips.at[1, :, 56:64, :], halo_corner.at[0]),
    )
    halo = [
        send(moves[i][0], moves[i][1], send_halo.at[i], recv_halo.at[i], around[i]) for i in (4, 5, 6, 7, 0, 1, 2, 3)
    ]

    lane = lanes(STEP)
    zero = jnp.zeros((STEP, 128), F32)

    def clear(i, _):
        for f in range(FRAMES):
            for p in range(3):
                for t in range(3):
                    spread[f, p, t, pl.ds(16 * i, 16), :] = zero
                    spread[f, p, t, pl.ds(LEAD + W + 16 * i, 16), :] = zero
        return 0

    lax.fori_loop(0, LEAD // 16, clear, 0)
    loads[1].wait()
    loads[2].wait()
    sums = jnp.zeros((8, 128), F32)
    for f in range(FRAMES):
        amp_loads[2 * f].wait()
        amp_loads[2 * f + 1].wait()
        parts = []
        for parity in (0, 1):
            a = jnp.concatenate([amps[f, t, pl.ds(parity, HALF, stride=2), :] for t in range(2)], axis=1)
            squares = a * a
            sums = sums + (squares[:, :128] + squares[:, 128:]).reshape(16, 8, 128).sum(axis=0)
            high = a.astype(BF16)
            rest = a - high.astype(F32)
            middle = rest.astype(BF16)
            low = (rest - middle.astype(F32)).astype(BF16)
            parts.append(jnp.concatenate([high, middle, low], axis=1))
        both = jnp.concatenate(parts, axis=0)
        sorter = sort[...]
        sorted_amp[f] = jnp.dot(
            both, jnp.concatenate([sorter, sorter, sorter], axis=0), preferred_element_type=F32
        )
    early0[pl.ds(W, 8), :] = sums

    at_row = [pos[0, 0, 0, f] for f in range(FRAMES)]
    at_col = [pos[0, 0, 1, f] for f in range(FRAMES)]

    def gather(f, p, row):
        b = at_col[f]
        tiles = [ext[p, t, pl.ds(at_row[f] + row, STEP), :] for t in range(3)]
        turned = [pltpu.roll(t, lax.rem(128 - b, 128), 1) for t in tiles]
        keep = lane < 128 - b
        return jnp.concatenate(
            [jnp.where(keep, turned[0], turned[1]), jnp.where(keep, turned[1], turned[2])], axis=1
        )

    def scatter(f, p, row, value):
        b = at_col[f]
        behind = lane >= b
        v0, v1 = pltpu.roll(value[:, :128], b, 1), pltpu.roll(value[:, 128:], b, 1)
        at = pl.ds(LEAD + row, STEP)
        spread[f, p, 0, at, :] = jnp.where(behind, v0, zero)
        spread[f, p, 1, at, :] = jnp.where(behind, v1, v0)
        spread[f, p, 2, at, :] = jnp.where(behind, zero, v1)

    for row in range(0, W, STEP):
        here = pl.ds(row, STEP)
        pr, pi = probe[0, here, :], probe[1, here, :]
        for f in range(FRAMES):
            scatter(f, 2, row, pr * pr + pi * pi)

    def gather_canvas(planes):
        def some(i, _):
            row = pl.multiple_of(16 * i, 16)
            for p in planes:
                for t in range(3):
                    total = spread[0, p, t, pl.ds(LEAD - at_row[0] + row, 16), :]
                    for f in range(1, FRAMES):
                        total = total + spread[f, p, t, pl.ds(LEAD - at_row[f] + row, 16), :]
                    canvas[p, t, pl.ds(row, 16), :] = total
            return 0

        lax.fori_loop(0, SIDE // 16, some, 0)

    gather_canvas((2,))
    loads[3].wait()

    lane8 = lanes()
    first = lane8 < 32
    second = lane8 < 64
    zero8 = jnp.zeros((8, 128), F32)
    has_n, has_s = r > 0, r < rows - 1
    has_w, has_e = c > 0, c < cols - 1

    def strip(ref, at, q, target, keep):
        amount = (target - 32 * q) % 128
        block = ref[at]
        block = pltpu.roll(block, amount, 1) if amount else block
        return jnp.where(keep, block, zero8)

    def put(p, row, centre, west, east):
        t0, t1 = pltpu.roll(centre[0], 32, 1), pltpu.roll(centre[1], 32, 1)
        ext[p, 0, pl.ds(row, 8), :] = jnp.where(first, west, t0)
        ext[p, 1, pl.ds(row, 8), :] = jnp.where(first, t0, t1)
        ext[p, 2, pl.ds(row, 8), :] = jnp.where(first, t1, jnp.where(second, east, zero8))

    for copy in halo:
        copy.wait_recv()
    for p in range(2):
        for k in range(4):
            for side, (keep_v, base) in enumerate(((has_n, 0), (has_s, MARGIN + W))):
                block = halo_ns[side, p, pl.ds(8 * k, 8), :]
                block = jnp.where(keep_v, block, jnp.zeros_like(block))
                west = strip(halo_corner, (2 * side, p, slice(0, 8)), k, 0, has_w & keep_v)
                east = strip(halo_corner, (2 * side + 1, p, slice(0, 8)), k, 32, has_e & keep_v)
                put(p, base + 8 * k, (block[:, :128], block[:, 128:]), west, east)
        for j in range(8):
            for q in range(4):
                at = 32 * j + 8 * q
                block = obj[p, pl.ds(at, 8), :]
                west = strip(halo_we, (0, p, pl.ds(8 * j, 8)), q, 0, has_w)
                east = strip(halo_we, (1, p, pl.ds(8 * j, 8)), q, 32, has_e)
                put(p, MARGIN + at, (block[:, :128], block[:, 128:]), west, east)

    def halve(f, stage, side, rows_at, value):
        h, l = split(value)
        half[f, stage, side, 0, rows_at, :] = h
        half[f, stage, side, 1, rows_at, :] = l

    for row in range(0, HALF, STEP):
        sums = [jnp.zeros((STEP, W), F32)] * 2
        for f in range(FRAMES):
            waves = []
            for i, base in enumerate((row, HALF + row)):
                here = pl.ds(base, STEP)
                wr, wi = gather(f, 0, base), gather(f, 1, base)
                pr, pi = probe[0, here, :], probe[1, here, :]
                win[f, 0, here, :] = wr
                win[f, 1, here, :] = wi
                sums[i] = sums[i] + (wr * wr + wi * wi)
                waves.append((pr * wr - pi * wi, pr * wi + pi * wr))
            for part in range(2):
                top, low = waves[0][part], waves[1][part]
                where = pl.ds(HALF * part + row, STEP)
                halve(f, 0, 0, where, top + low)
                halve(f, 0, 1, where, top - low)
        for i, base in enumerate((row, HALF + row)):
            power2[pl.ds(base, STEP), :] = sums[i][:, :128]
            power2[pl.ds(W + base, STEP), :] = sums[i][:, 128:]

    mine8 = pl.multiple_of(core * HALF, HALF)
    other8 = pl.multiple_of((1 - core) * HALF, HALF)
    for t in range(2):
        early0[pl.ds(HALF * t, HALF), :] = power2[pl.ds(W * t + other8, HALF), :]
    e0 = send(early0, early0_got, send_pair.at[0], recv_pair.at[0], pair)

    def left_dots(stage, flip):
        for f in range(FRAMES):
            for side in range(2):
                mid[f, stage, side] = triple(
                    (table[flip + side, 0], table[flip + side, 1]),
                    (half[f, stage, side, 0], half[f, stage, side, 1]),
                )

    def right_dots(stage, flip):
        for f in range(FRAMES):
            for side in range(2):
                mid[f, stage, side] = triple(
                    (half[f, stage, side, 0], half[f, stage, side, 1]),
                    (table[flip + side, 0], table[flip + side, 1]),
                )

    left_dots(0, 0)
    for f in range(FRAMES):
        for parity in range(2):
            for row in range(0, HALF, STEP):
                zr = mid[f, 0, parity, pl.ds(row, STEP), :]
                zi = mid[f, 0, parity, pl.ds(HALF + row, STEP), :]
                here = pl.ds(HALF * parity + row, STEP)
                plus = jnp.concatenate([zr[:, :128] + zr[:, 128:], zi[:, :128] + zi[:, 128:]], axis=1)
                less = jnp.concatenate([zr[:, :128] - zr[:, 128:], zi[:, :128] - zi[:, 128:]], axis=1)
                halve(f, 1, 0, here, plus)
                halve(f, 1, 1, here, less)

    k = 4 * x + y
    e0.wait_recv()
    for i in range(16):
        for t in range(2):
            at = mine8 + 8 * i
            early1[i, pl.ds(8 * t, 8), :] = (
                power2[pl.ds(W * t + at, 8), :] + early0_got[pl.ds(HALF * t + 8 * i, 8), :]
            )
        early1[i, pl.ds(16, 8), :] = early0[pl.ds(W, 8), :] + early0_got[pl.ds(W, 8), :]
    early1_got[k] = early1[k]
    e1 = []
    for i, (x_, y_) in enumerate(on_plane):
        e1.append(send(early1.at[4 * x_ + y_], early1_got.at[k], send_e1.at[i], recv_e1.at[k], plane[i]))

    right_dots(1, 2)
    for f in range(FRAMES):
        for side in range(2):
            for row in range(0, W, STEP):
                here = pl.ds(row, STEP)
                amp = sorted_amp[f, here, 128 * side : 128 * side + 128]
                v = mid[f, 1, side, here, :]
                zr, zi = v[:, :128], v[:, 128:]
                factor = amp * lax.rsqrt(zr * zr + zi * zi + smoothing)
                halve(f, 2, side, here, jnp.concatenate([zr * factor, zi * factor], axis=1))

    right_dots(2, 0)

    def arrive(dst, recvs):
        pltpu.make_async_remote_copy(
            src_ref=dst, dst_ref=dst, send_sem=recvs, recv_sem=recvs, device_id=pair, device_id_type=MESH
        ).wait_recv()

    for x_, y_ in behind_plane:
        arrive(early1_got.at[4 * x_ + y_], recv_e1.at[4 * x_ + y_])
    total = early1_got[0]
    for i in range(1, 16):
        total = total + early1_got[i]
    early2[z] = total
    e2 = [send(early2.at[z], early2.at[z], send_e2.at[i], recv_e2.at[z], column[i]) for i in range(7)]

    for f in range(FRAMES):
        for parity in range(2):
            for row in range(0, HALF, STEP):
                here = pl.ds(HALF * parity + row, STEP)
                even, odd = mid[f, 2, 0, here, :], mid[f, 2, 1, here, :]
                plus, less = even + odd, even - odd
                for part in range(2):
                    cut = slice(128 * part, 128 * part + 128)
                    value = jnp.concatenate([plus[:, cut], less[:, cut]], axis=1)
                    halve(f, 3, parity, pl.ds(HALF * part + row, STEP), value)

    left_dots(3, 2)
    for row in range(0, HALF, STEP):
        parts = []
        for f in range(FRAMES):
            er, orr = mid[f, 3, 0, pl.ds(row, STEP), :], mid[f, 3, 1, pl.ds(row, STEP), :]
            ei, oi = mid[f, 3, 0, pl.ds(HALF + row, STEP), :], mid[f, 3, 1, pl.ds(HALF + row, STEP), :]
            parts.append(((er + orr, ei + oi), (er - orr, ei - oi)))
        for side, base in enumerate((row, HALF + row)):
            here = pl.ds(base, STEP)
            pr, pi = probe[0, here, :], probe[1, here, :]
            sums = [jnp.zeros((STEP, W), F32)] * 2
            for f in range(FRAMES):
                wr, wi = win[f, 0, here, :], win[f, 1, here, :]
                dr = parts[f][side][0] - (pr * wr - pi * wi)
                di = parts[f][side][1] - (pr * wi + pi * wr)
                scatter(f, 0, base, pr * dr + pi * di)
                scatter(f, 1, base, pr * di - pi * dr)
                sums = [sums[0] + (wr * dr + wi * di), sums[1] + (wr * di - wi * dr)]
            acc[0, here, :], acc[1, here, :] = sums

    mine = pl.ds(mine8, HALF)
    other = pl.ds(other8, HALF)
    c0 = send(acc.at[:, other, :], got0, send_pair.at[1], recv_pair.at[1], pair)

    gather_canvas((0, 1))
    for p in range(3):
        for side, base in enumerate((0, MARGIN + W)):
            for q in range(4):
                t = [pltpu.roll(canvas[p, i, pl.ds(base + 8 * q, 8), :], 96, 1) for i in range(3)]
                bands[side, p, pl.ds(8 * q, 8), 0:128] = jnp.where(lane8 < 96, t[0], t[1])
                bands[side, p, pl.ds(8 * q, 8), 128:256] = jnp.where(lane8 < 96, t[1], t[2])

    c0.wait_recv()
    for p in range(2):
        part0[p] = acc[p, mine, :] + got0[p]
    c1 = []
    for i, (x_, y_) in enumerate(on_plane):
        src = part0.at[:, pl.ds(pl.multiple_of(8 * (4 * x_ + y_), 8), 8), :]
        c1.append(send(src, got1.at[i], send_m1.at[i], recv_m1.at[i], plane[i]))

    for p in range(3):
        for j in range(10):
            left = [canvas[p, 0, pl.ds(32 * j + 8 * q, 8), :] for q in range(4)]
            right = [canvas[p, 2, pl.ds(32 * j + 8 * q, 8), :] for q in range(4)]
            strips[0, p, pl.ds(8 * j, 8), :] = pack(left, 0)
            strips[1, p, pl.ds(8 * j, 8), :] = pack(right, 96)

    own = pl.ds(pl.multiple_of(8 * k, 8), 8)
    for copy in c1:
        copy.wait_recv()
    total = part0[:, own, :]
    for i in range(15):
        total = total + got1[i]
    all2[z] = total
    c2 = [send(all2.at[z], all2.at[z], send_m2.at[i], recv_m2.at[z], column[i]) for i in range(7)]

    moves = (
        (bands.at[0], from_ns.at[1]),
        (bands.at[1], from_ns.at[0]),
        (strips.at[0, :, 8:72, :], from_we.at[1]),
        (strips.at[1, :, 8:72, :], from_we.at[0]),
        (strips.at[0, :, 0:8, :], from_corner.at[3]),
        (strips.at[1, :, 0:8, :], from_corner.at[2]),
        (strips.at[0, :, 72:80, :], from_corner.at[1]),
        (strips.at[1, :, 72:80, :], from_corner.at[0]),
    )
    edges = [
        send(moves[i][0], moves[i][1], send_edge.at[i], recv_edge.at[i], around[i]) for i in (4, 5, 6, 7, 0, 1, 2, 3)
    ]

    for d in range(1, 8):
        arrive(early2.at[lax.rem(z + d, 8)], recv_e2.at[lax.rem(z + d, 8)])
    total = early2[0]
    for i in range(1, 8):
        total = total + early2[i]
    weight = 1.0 / (jnp.concatenate([total[0:8], total[8:16]], axis=1) + regular)
    target = jnp.sum(total[16:24]) * (1.0 / (FRAMES * rows * cols))

    block = pl.ds(pl.multiple_of(HALF * core + 8 * k, 8), 8)
    for d in range(1, 8):
        arrive(all2.at[lax.rem(z + d, 8)], recv_m2.at[lax.rem(z + d, 8)])
    total = all2[0]
    for i in range(1, 8):
        total = total + all2[i]
    for p in range(2):
        gathered[p, block, :] = probe[p, block, :] + total[p] * weight
    g1 = [
        send(gathered.at[:, block, :], gathered.at[:, block, :], send_ag.at[i], recv_ag.at[i], plane[i])
        for i in range(15)
    ]
    fw = [send(gathered.at[:, block, :], gathered.at[:, block, :], send_fw.at[15], recv_fw.at[15], pair)]

    for copy in edges:
        copy.wait_recv()
    for j in range(8):
        for q in range(4):
            at = 32 * j + 8 * q
            totals = []
            for p in range(3):
                t = [pltpu.roll(canvas[p, i, pl.ds(MARGIN + at, 8), :], 96, 1) for i in range(3)]
                left = jnp.where(lane8 < 96, t[0], t[1])
                right = jnp.where(lane8 < 96, t[1], t[2])
                if j in (0, 7):
                    side = 0 if j == 0 else 1
                    keep_v = has_n if j == 0 else has_s
                    band = from_ns[side, p, pl.ds(8 * q, 8), :]
                    left = left + jnp.where(keep_v, band[:, :128], zero8)
                    right = right + jnp.where(keep_v, band[:, 128:], zero8)
                    west = strip(from_corner, (2 * side, p, slice(0, 8)), q, 0, has_w & keep_v)
                    east = strip(from_corner, (2 * side + 1, p, slice(0, 8)), q, 96, has_e & keep_v)
                    left = left + jnp.where(first, west, zero8)
                    right = right + jnp.where(lane8 >= 96, east, zero8)
                west = strip(from_we, (0, p, pl.ds(8 * j, 8)), q, 0, has_w)
                east = strip(from_we, (1, p, pl.ds(8 * j, 8)), q, 96, has_e)
                left = left + jnp.where(first, west, zero8)
                right = right + jnp.where(lane8 >= 96, east, zero8)
                totals.append((left, right))
            for s in range(2):
                scale = 1.0 / (totals[2][s] + regular)
                for p in range(2):
                    here = (p, pl.ds(at, 8), slice(128 * s, 128 * s + 128))
                    out_obj[here] = obj[here] + totals[p][s] * scale

    for i in reversed(range(15)):
        x_, y_ = behind_plane[i]
        at = pl.ds(pl.multiple_of(HALF * core + 8 * (4 * x_ + y_), 8), 8)
        arrive(gathered.at[:, at, :], recv_ag.at[i])
        fw.append(send(gathered.at[:, at, :], gathered.at[:, at, :], send_fw.at[i], recv_fw.at[i], pair))
    for i in range(16):
        x_, y_ = behind_plane[i] if i < 15 else (x, y)
        at = pl.ds(pl.multiple_of(HALF * (1 - core) + 8 * (4 * x_ + y_), 8), 8)
        arrive(gathered.at[:, at, :], recv_fw.at[i])
    power = jnp.zeros((8, W), F32)
    for p in range(2):
        g = gathered[p]
        power = power + (g * g).reshape(32, 8, W).sum(axis=0)
    scale = jnp.sqrt(jnp.full((8, W), target, F32) / (jnp.sum(power) + epsilon))
    for p in range(2):
        out_probe[p] = gathered[p] * jnp.concatenate([scale] * 32, axis=0)

    for copy in halo + [e0, c0] + e1 + e2 + c1 + c2 + edges + g1 + fw:
        copy.wait_send()


def vmem(*shape, dtype=F32):
    return pltpu.VMEM(shape, dtype)


def per_device(rows, cols, object_field, probe, amplitudes, positions):
    in_vmem = pl.BlockSpec(memory_space=pltpu.VMEM)
    in_smem = pl.BlockSpec(memory_space=pltpu.SMEM)
    in_hbm = pl.BlockSpec(memory_space=pl.ANY)
    dma = pltpu.SemaphoreType.DMA
    return pl.pallas_call(
        functools.partial(kernel, rows, cols),
        out_shape=(jax.ShapeDtypeStruct((2, W, W), F32),) * 2,
        in_specs=[in_smem] + [in_hbm] * 5,
        out_specs=(in_vmem,) * 2,
        scratch_shapes=[
            vmem(2, W, W),
            vmem(2, W, W),
            vmem(FRAMES, 2, W, 128),
            vmem(4, 2, W, W, dtype=BF16),
            vmem(W, W, dtype=BF16),
            vmem(2, 2, 64, 128),
            vmem(2, 2, 32, W),
            vmem(2, 2, 64, 128),
            vmem(4, 2, 8, 128),
            vmem(2, 3, SIDE, 128),
            vmem(FRAMES, 3, 3, LEAD + W + LEAD, 128),
            vmem(FRAMES, 2, W, W),
            vmem(FRAMES, W, W),
            vmem(FRAMES, 4, 2, 2, W, W, dtype=BF16),
            vmem(FRAMES, 4, 2, W, W),
            vmem(2, W, W),
            vmem(2 * W, 128),
            vmem(3, 3, SIDE, 128),
            vmem(2, 3, 80, 128),
            vmem(2, 3, 32, W),
            vmem(2, 3, 32, W),
            vmem(2, 3, 64, 128),
            vmem(4, 3, 8, 128),
            vmem(W + 8, 128),
            vmem(W + 8, 128),
            vmem(16, 24, 128),
            vmem(16, 24, 128),
            vmem(8, 24, 128),
            vmem(2, HALF, W),
            vmem(2, HALF, W),
            vmem(15, 2, 8, W),
            vmem(8, 2, 8, W),
            vmem(2, W, W),
            dma((4,)),
            dma((2 * FRAMES,)),
            dma((8,)),
            dma((8,)),
            dma((8,)),
            dma((8,)),
            dma((2,)),
            dma((2,)),
            dma((15,)),
            dma((16,)),
            dma((7,)),
            dma((8,)),
            dma((15,)),
            dma((15,)),
            dma((7,)),
            dma((8,)),
            dma((15,)),
            dma((15,)),
            dma((16,)),
            dma((16,)),
        ],
        compiler_params=pltpu.CompilerParams(
            collective_id=0, has_side_effects=True, vmem_limit_bytes=56 * 2**20
        ),
        name="ptycho",
    )(
        jnp.swapaxes(positions, 2, 3),
        object_field,
        probe,
        amplitudes,
        jnp.asarray(dft_tables()),
        jnp.asarray(sort_table()),
    )


def solution(mesh):
    return jax.shard_map(
        functools.partial(per_device, mesh.shape["row"], mesh.shape["col"]),
        mesh=mesh,
        in_specs=(
            P(None, "row", "col"),
            P(),
            P("row", "col", None, None, None),
            P("row", "col", None, None),
        ),
        out_specs=(P(None, "row", "col"), P()),
        check_vma=False,
    )
```

```python
import functools
import math

import jax
import jax.numpy as jnp
import numpy as np
from jax import lax
from jax.experimental import pallas as pl
from jax.experimental.pallas import tpu as pltpu
from jax.sharding import PartitionSpec as P

W = 256
HALF = W // 2
MARGIN = 32
FRAMES = 4
SIDE = W + 2 * MARGIN
LEAD = 2 * MARGIN

smoothing = 0.1
regular = 1.0
epsilon = 1e-06

MESH = pl.DeviceIdType.MESH
F32 = jnp.float32
BF16 = jnp.bfloat16

COMPASS = ((-1, 0), (1, 0), (0, -1), (0, 1), (-1, -1), (-1, 1), (1, -1), (1, 1))


def dft_tables():
    k = np.arange(HALF)
    j = np.arange(HALF)
    mats = []
    for parity in (0, 1):
        phase = (2 * k[:, None] + parity) * j[None, :] % W
        z = np.exp(-2j * np.pi * phase / W) / math.sqrt(W)
        mats.append(np.block([[z.real, -z.imag], [z.imag, z.real]]))
    mats += [m.T for m in mats]
    full = np.stack(mats)
    high = full.astype(BF16)
    low = (full - high.astype(np.float64)).astype(BF16)
    return np.stack([high, low], 1)


def sort_table():
    table = np.zeros((W, W), np.float32)
    k = np.arange(HALF)
    table[2 * k, k] = 1
    table[2 * k + 1, HALF + k] = 1
    return table.astype(BF16)


def split(x):
    high = x.astype(BF16)
    return high, (x - high.astype(F32)).astype(BF16)


def lanes(rows=8):
    return lax.broadcasted_iota(jnp.int32, (rows, 128), 1)


def neighbours(r, c, rows, cols):
    return [(lax.rem(r + dr + rows, rows), lax.rem(c + dc + cols, cols)) for dr, dc in COMPASS]


def pack(blocks, shift):
    group = lanes() // 32
    out = None
    for q, block in enumerate(blocks):
        amount = (shift + 32 * q) % 128
        turned = pltpu.roll(block, amount, 1) if amount else block
        out = turned if out is None else jnp.where(group == q, turned, out)
    return out


STEP = 16


def triple(left, right):
    a = jnp.concatenate([left[0], left[0], left[1]], axis=1)
    b = jnp.concatenate([right[0], right[1], right[0]], axis=0)
    return jnp.dot(a, b, preferred_element_type=F32)


def send(src, dst, sends, recvs, device):
    copy = pltpu.make_async_remote_copy(
        src_ref=src, dst_ref=dst, send_sem=sends, recv_sem=recvs, device_id=device, device_id_type=MESH
    )
    copy.start()
    return copy


def kernel(
    rows,
    cols,
    pos_hbm,
    obj_hbm,
    probe_hbm,
    amps_hbm,
    table_hbm,
    sort_hbm,
    out_obj,
    out_probe,
    pos,
    obj,
    probe,
    amps,
    table,
    sort,
    halo_strips,
    halo_ns,
    halo_we,
    halo_corner,
    ext,
    spread,
    win,
    sorted_amp,
    half,
    mid,
    acc,
    power2,
    canvas,
    strips,
    bands,
    from_ns,
    from_we,
    from_corner,
    early0,
    early0_got,
    early1,
    early1_got,
    early2,
    got0,
    part0,
    got1,
    all2,
    gathered,
    load_sem,
    amp_sem,
    send_halo,
    recv_halo,
    send_edge,
    recv_edge,
    send_pair,
    recv_pair,
    send_e1,
    recv_e1,
    send_e2,
    recv_e2,
    send_m1,
    recv_m1,
    send_m2,
    recv_m2,
    send_ag,
    recv_ag,
    send_fw,
    recv_fw,
):
    loads = [
        pltpu.make_async_copy(src, dst, load_sem.at[i])
        for i, (src, dst) in enumerate(
            ((obj_hbm, obj), (probe_hbm, probe), (sort_hbm, sort), (table_hbm, table), (pos_hbm, pos))
        )
    ]
    loads[0].start()
    amp_loads = []
    for f in range(FRAMES):
        for t in range(2):
            amp_loads.append(
                pltpu.make_async_copy(
                    amps_hbm.at[0, 0, f, :, 128 * t : 128 * t + 128], amps.at[f, t], amp_sem.at[2 * f + t]
                )
            )

    r, c = lax.axis_index("row"), lax.axis_index("col")
    core, x, y_lo = lax.rem(c, 2), lax.rem(c // 2, 4), c // 8
    y_hi, z = lax.rem(r, 2), r // 2
    y = 2 * y_hi + y_lo

    def place(core_, x_, y_, z_):
        return (2 * z_ + y_ // 2, (lax.rem(y_, 2) * 4 + x_) * 2 + core_)

    around = neighbours(r, c, rows, cols)
    pair = place(1 - core, x, y, z)
    steps_xy = [(2, 2), (1, 2), (3, 2), (2, 1), (2, 3), (1, 1), (1, 3), (3, 1), (3, 3), (2, 0), (0, 2), (1, 0), (3, 0), (0, 1), (0, 3)]
    on_plane = [(lax.rem(x + dx, 4), lax.rem(y + dy, 4)) for dx, dy in steps_xy]
    behind_plane = [(lax.rem(x + 4 - dx, 4), lax.rem(y + 4 - dy, 4)) for dx, dy in steps_xy]
    plane = [place(core, x_, y_, z) for x_, y_ in on_plane]
    steps_z = [4, 3, 5, 2, 6, 1, 7]
    column = [place(core, x, y, lax.rem(z + d, 8)) for d in steps_z]
    everyone = around + [pair] + plane + column
    barrier = pltpu.get_barrier_semaphore()
    for partner in everyone:
        pl.semaphore_signal(barrier, inc=1, device_id=partner, device_id_type=MESH)
    loads[1].start()
    loads[4].start()
    loads[2].start()
    for load in amp_loads:
        load.start()
    loads[3].start()

    loads[0].wait()
    for p in range(2):
        for j in range(8):
            left = [obj[p, pl.ds(32 * j + 8 * q, 8), 0:128] for q in range(4)]
            right = [obj[p, pl.ds(32 * j + 8 * q, 8), 128:256] for q in range(4)]
            halo_strips[0, p, pl.ds(8 * j, 8), :] = pack(left, 0)
            halo_strips[1, p, pl.ds(8 * j, 8), :] = pack(right, 32)
    pl.semaphore_wait(barrier, len(everyone))
    moves = (
        (obj.at[:, 0:32, :], halo_ns.at[1]),
        (obj.at[:, W - 32 : W, :], halo_ns.at[0]),
        (halo_strips.at[0], halo_we.at[1]),
        (halo_strips.at[1], halo_we.at[0]),
        (halo_strips.at[0, :, 0:8, :], halo_corner.at[3]),
        (halo_strips.at[1, :, 0:8, :], halo_corner.at[2]),
        (halo_strips.at[0, :, 56:64, :], halo_corner.at[1]),
        (halo_strips.at[1, :, 56:64, :], halo_corner.at[0]),
    )
    halo = [
        send(moves[i][0], moves[i][1], send_halo.at[i], recv_halo.at[i], around[i]) for i in (4, 5, 6, 7, 0, 1, 2, 3)
    ]

    lane = lanes(STEP)
    zero = jnp.zeros((STEP, 128), F32)

    def clear(i, _):
        for f in range(FRAMES):
            for p in range(3):
                for t in range(3):
                    spread[f, p, t, pl.ds(16 * i, 16), :] = zero
                    spread[f, p, t, pl.ds(LEAD + W + 16 * i, 16), :] = zero
        return 0

    lax.fori_loop(0, LEAD // 16, clear, 0)
    loads[1].wait()
    loads[4].wait()
    loads[2].wait()
    sums = jnp.zeros((8, 128), F32)
    for f in range(FRAMES):
        amp_loads[2 * f].wait()
        amp_loads[2 * f + 1].wait()
        parts = []
        for parity in (0, 1):
            a = jnp.concatenate([amps[f, t, pl.ds(parity, HALF, stride=2), :] for t in range(2)], axis=1)
            squares = a * a
            sums = sums + (squares[:, :128] + squares[:, 128:]).reshape(16, 8, 128).sum(axis=0)
            high = a.astype(BF16)
            rest = a - high.astype(F32)
            middle = rest.astype(BF16)
            low = (rest - middle.astype(F32)).astype(BF16)
            parts.append(jnp.concatenate([high, middle, low], axis=1))
        both = jnp.concatenate(parts, axis=0)
        sorter = sort[...]
        sorted_amp[f] = jnp.dot(
            both, jnp.concatenate([sorter, sorter, sorter], axis=0), preferred_element_type=F32
        )
    early0[pl.ds(W, 8), :] = sums

    at_row = [pos[0, 0, 0, f] for f in range(FRAMES)]
    at_col = [pos[0, 0, 1, f] for f in range(FRAMES)]

    def gather(f, p, row):
        b = at_col[f]
        tiles = [ext[p, t, pl.ds(at_row[f] + row, STEP), :] for t in range(3)]
        turned = [pltpu.roll(t, lax.rem(128 - b, 128), 1) for t in tiles]
        keep = lane < 128 - b
        return jnp.concatenate(
            [jnp.where(keep, turned[0], turned[1]), jnp.where(keep, turned[1], turned[2])], axis=1
        )

    def scatter(f, p, row, value):
        b = at_col[f]
        behind = lane >= b
        v0, v1 = pltpu.roll(value[:, :128], b, 1), pltpu.roll(value[:, 128:], b, 1)
        at = pl.ds(LEAD + row, STEP)
        spread[f, p, 0, at, :] = jnp.where(behind, v0, zero)
        spread[f, p, 1, at, :] = jnp.where(behind, v1, v0)
        spread[f, p, 2, at, :] = jnp.where(behind, zero, v1)

    for row in range(0, W, STEP):
        here = pl.ds(row, STEP)
        pr, pi = probe[0, here, :], probe[1, here, :]
        for f in range(FRAMES):
            scatter(f, 2, row, pr * pr + pi * pi)

    def gather_canvas(planes):
        def some(i, _):
            row = pl.multiple_of(16 * i, 16)
            for p in planes:
                for t in range(3):
                    total = spread[0, p, t, pl.ds(LEAD - at_row[0] + row, 16), :]
                    for f in range(1, FRAMES):
                        total = total + spread[f, p, t, pl.ds(LEAD - at_row[f] + row, 16), :]
                    canvas[p, t, pl.ds(row, 16), :] = total
            return 0

        lax.fori_loop(0, SIDE // 16, some, 0)

    lane8 = lanes()
    first = lane8 < 32
    second = lane8 < 64
    zero8 = jnp.zeros((8, 128), F32)
    has_n, has_s = r > 0, r < rows - 1
    has_w, has_e = c > 0, c < cols - 1

    def strip(ref, at, q, target, keep):
        amount = (target - 32 * q) % 128
        block = ref[at]
        block = pltpu.roll(block, amount, 1) if amount else block
        return jnp.where(keep, block, zero8)

    def pack_edges(planes):
        for p in planes:
            for side, base in enumerate((0, MARGIN + W)):
                for q in range(4):
                    t = [pltpu.roll(canvas[p, i, pl.ds(base + 8 * q, 8), :], 96, 1) for i in range(3)]
                    bands[side, p, pl.ds(8 * q, 8), 0:128] = jnp.where(lane8 < 96, t[0], t[1])
                    bands[side, p, pl.ds(8 * q, 8), 128:256] = jnp.where(lane8 < 96, t[1], t[2])
            for j in range(10):
                left = [canvas[p, 0, pl.ds(32 * j + 8 * q, 8), :] for q in range(4)]
                right = [canvas[p, 2, pl.ds(32 * j + 8 * q, 8), :] for q in range(4)]
                strips[0, p, pl.ds(8 * j, 8), :] = pack(left, 0)
                strips[1, p, pl.ds(8 * j, 8), :] = pack(right, 96)

    def send_edges(planes, base):
        at = pl.ds(planes[0], len(planes))
        moves = (
            (bands.at[0, at], from_ns.at[1, at]),
            (bands.at[1, at], from_ns.at[0, at]),
            (strips.at[0, at, 8:72, :], from_we.at[1, at]),
            (strips.at[1, at, 8:72, :], from_we.at[0, at]),
            (strips.at[0, at, 0:8, :], from_corner.at[3, at]),
            (strips.at[1, at, 0:8, :], from_corner.at[2, at]),
            (strips.at[0, at, 72:80, :], from_corner.at[1, at]),
            (strips.at[1, at, 72:80, :], from_corner.at[0, at]),
        )
        return [
            send(moves[i][0], moves[i][1], send_edge.at[base + i], recv_edge.at[base + i], around[i])
            for i in (4, 5, 6, 7, 0, 1, 2, 3)
        ]

    gather_canvas((2,))
    pack_edges((2,))
    loads[3].wait()

    def put(p, row, centre, west, east):
        t0, t1 = pltpu.roll(centre[0], 32, 1), pltpu.roll(centre[1], 32, 1)
        ext[p, 0, pl.ds(row, 8), :] = jnp.where(first, west, t0)
        ext[p, 1, pl.ds(row, 8), :] = jnp.where(first, t0, t1)
        ext[p, 2, pl.ds(row, 8), :] = jnp.where(first, t1, jnp.where(second, east, zero8))

    for copy in halo:
        copy.wait_recv()
    for p in range(2):
        for k in range(4):
            for side, (keep_v, base) in enumerate(((has_n, 0), (has_s, MARGIN + W))):
                block = halo_ns[side, p, pl.ds(8 * k, 8), :]
                block = jnp.where(keep_v, block, jnp.zeros_like(block))
                west = strip(halo_corner, (2 * side, p, slice(0, 8)), k, 0, has_w & keep_v)
                east = strip(halo_corner, (2 * side + 1, p, slice(0, 8)), k, 32, has_e & keep_v)
                put(p, base + 8 * k, (block[:, :128], block[:, 128:]), west, east)
        for j in range(8):
            for q in range(4):
                at = 32 * j + 8 * q
                block = obj[p, pl.ds(at, 8), :]
                west = strip(halo_we, (0, p, pl.ds(8 * j, 8)), q, 0, has_w)
                east = strip(halo_we, (1, p, pl.ds(8 * j, 8)), q, 32, has_e)
                put(p, MARGIN + at, (block[:, :128], block[:, 128:]), west, east)

    edges = send_edges((2,), 0)

    def halve(f, stage, side, rows_at, value):
        h, l = split(value)
        half[f, stage, side, 0, rows_at, :] = h
        half[f, stage, side, 1, rows_at, :] = l

    for row in range(0, HALF, STEP):
        sums = [jnp.zeros((STEP, W), F32)] * 2
        for f in range(FRAMES):
            waves = []
            for i, base in enumerate((row, HALF + row)):
                here = pl.ds(base, STEP)
                wr, wi = gather(f, 0, base), gather(f, 1, base)
                pr, pi = probe[0, here, :], probe[1, here, :]
                win[f, 0, here, :] = wr
                win[f, 1, here, :] = wi
                sums[i] = sums[i] + (wr * wr + wi * wi)
                waves.append((pr * wr - pi * wi, pr * wi + pi * wr))
            for part in range(2):
                top, low = waves[0][part], waves[1][part]
                where = pl.ds(HALF * part + row, STEP)
                halve(f, 0, 0, where, top + low)
                halve(f, 0, 1, where, top - low)
        for i, base in enumerate((row, HALF + row)):
            power2[pl.ds(base, STEP), :] = sums[i][:, :128]
            power2[pl.ds(W + base, STEP), :] = sums[i][:, 128:]

    mine8 = pl.multiple_of(core * HALF, HALF)
    other8 = pl.multiple_of((1 - core) * HALF, HALF)
    for t in range(2):
        early0[pl.ds(HALF * t, HALF), :] = power2[pl.ds(W * t + other8, HALF), :]
    e0 = send(early0, early0_got, send_pair.at[0], recv_pair.at[0], pair)

    def left_dots(stage, flip):
        for f in range(FRAMES):
            for side in range(2):
                mid[f, stage, side] = triple(
                    (table[flip + side, 0], table[flip + side, 1]),
                    (half[f, stage, side, 0], half[f, stage, side, 1]),
                )

    def right_dots(stage, flip):
        for f in range(FRAMES):
            for side in range(2):
                mid[f, stage, side] = triple(
                    (half[f, stage, side, 0], half[f, stage, side, 1]),
                    (table[flip + side, 0], table[flip + side, 1]),
                )

    left_dots(0, 0)
    for f in range(FRAMES):
        for parity in range(2):
            for row in range(0, HALF, STEP):
                zr = mid[f, 0, parity, pl.ds(row, STEP), :]
                zi = mid[f, 0, parity, pl.ds(HALF + row, STEP), :]
                here = pl.ds(HALF * parity + row, STEP)
                plus = jnp.concatenate([zr[:, :128] + zr[:, 128:], zi[:, :128] + zi[:, 128:]], axis=1)
                less = jnp.concatenate([zr[:, :128] - zr[:, 128:], zi[:, :128] - zi[:, 128:]], axis=1)
                halve(f, 1, 0, here, plus)
                halve(f, 1, 1, here, less)

    k = 4 * x + y
    e0.wait_recv()
    for i in range(16):
        for t in range(2):
            at = mine8 + 8 * i
            early1[i, pl.ds(8 * t, 8), :] = (
                power2[pl.ds(W * t + at, 8), :] + early0_got[pl.ds(HALF * t + 8 * i, 8), :]
            )
        early1[i, pl.ds(16, 8), :] = early0[pl.ds(W, 8), :] + early0_got[pl.ds(W, 8), :]
    early1_got[k] = early1[k]
    e1 = []
    for i, (x_, y_) in enumerate(on_plane):
        e1.append(send(early1.at[4 * x_ + y_], early1_got.at[k], send_e1.at[i], recv_e1.at[k], plane[i]))

    right_dots(1, 2)
    for f in range(FRAMES):
        for side in range(2):
            for row in range(0, W, STEP):
                here = pl.ds(row, STEP)
                amp = sorted_amp[f, here, 128 * side : 128 * side + 128]
                v = mid[f, 1, side, here, :]
                zr, zi = v[:, :128], v[:, 128:]
                factor = amp * lax.rsqrt(zr * zr + zi * zi + smoothing)
                halve(f, 2, side, here, jnp.concatenate([zr * factor, zi * factor], axis=1))

    right_dots(2, 0)

    def arrive(dst, recvs):
        pltpu.make_async_remote_copy(
            src_ref=dst, dst_ref=dst, send_sem=recvs, recv_sem=recvs, device_id=pair, device_id_type=MESH
        ).wait_recv()

    for f in range(FRAMES):
        for parity in range(2):
            for row in range(0, HALF, STEP):
                here = pl.ds(HALF * parity + row, STEP)
                even, odd = mid[f, 2, 0, here, :], mid[f, 2, 1, here, :]
                plus, less = even + odd, even - odd
                for part in range(2):
                    cut = slice(128 * part, 128 * part + 128)
                    value = jnp.concatenate([plus[:, cut], less[:, cut]], axis=1)
                    halve(f, 3, parity, pl.ds(HALF * part + row, STEP), value)

    left_dots(3, 2)
    for row in range(0, HALF, STEP):
        parts = []
        for f in range(FRAMES):
            er, orr = mid[f, 3, 0, pl.ds(row, STEP), :], mid[f, 3, 1, pl.ds(row, STEP), :]
            ei, oi = mid[f, 3, 0, pl.ds(HALF + row, STEP), :], mid[f, 3, 1, pl.ds(HALF + row, STEP), :]
            parts.append(((er + orr, ei + oi), (er - orr, ei - oi)))
        for side, base in enumerate((row, HALF + row)):
            here = pl.ds(base, STEP)
            pr, pi = probe[0, here, :], probe[1, here, :]
            sums = [jnp.zeros((STEP, W), F32)] * 2
            for f in range(FRAMES):
                wr, wi = win[f, 0, here, :], win[f, 1, here, :]
                dr = parts[f][side][0] - (pr * wr - pi * wi)
                di = parts[f][side][1] - (pr * wi + pi * wr)
                scatter(f, 0, base, pr * dr + pi * di)
                scatter(f, 1, base, pr * di - pi * dr)
                sums = [sums[0] + (wr * dr + wi * di), sums[1] + (wr * di - wi * dr)]
            acc[0, here, :], acc[1, here, :] = sums

    mine = pl.ds(mine8, HALF)
    other = pl.ds(other8, HALF)
    c0 = send(acc.at[:, other, :], got0, send_pair.at[1], recv_pair.at[1], pair)

    gather_canvas((0, 1))

    c0.wait_recv()
    for p in range(2):
        part0[p] = acc[p, mine, :] + got0[p]
    c1 = []
    for i, (x_, y_) in enumerate(on_plane):
        src = part0.at[:, pl.ds(pl.multiple_of(8 * (4 * x_ + y_), 8), 8), :]
        c1.append(send(src, got1.at[i], send_m1.at[i], recv_m1.at[i], plane[i]))

    pack_edges((0, 1))
    for x_, y_ in behind_plane:
        arrive(early1_got.at[4 * x_ + y_], recv_e1.at[4 * x_ + y_])
    total = early1_got[0]
    for i in range(1, 16):
        total = total + early1_got[i]
    early2[z] = total
    e2 = [send(early2.at[z], early2.at[z], send_e2.at[i], recv_e2.at[z], column[i]) for i in range(7)]

    own = pl.ds(pl.multiple_of(8 * k, 8), 8)
    for copy in c1:
        copy.wait_recv()
    total = part0[:, own, :]
    for i in range(15):
        total = total + got1[i]
    all2[z] = total
    c2 = [send(all2.at[z], all2.at[z], send_m2.at[i], recv_m2.at[z], column[i]) for i in range(7)]

    edges += send_edges((0, 1), 8)

    for d in range(1, 8):
        arrive(early2.at[lax.rem(z + d, 8)], recv_e2.at[lax.rem(z + d, 8)])
    total = early2[0]
    for i in range(1, 8):
        total = total + early2[i]
    weight = 1.0 / (jnp.concatenate([total[0:8], total[8:16]], axis=1) + regular)
    target = jnp.sum(total[16:24]) * (1.0 / (FRAMES * rows * cols))

    block = pl.ds(pl.multiple_of(HALF * core + 8 * k, 8), 8)
    for d in range(1, 8):
        arrive(all2.at[lax.rem(z + d, 8)], recv_m2.at[lax.rem(z + d, 8)])
    total = all2[0]
    for i in range(1, 8):
        total = total + all2[i]
    for p in range(2):
        gathered[p, block, :] = probe[p, block, :] + total[p] * weight
    g1 = [
        send(gathered.at[:, block, :], gathered.at[:, block, :], send_ag.at[i], recv_ag.at[i], plane[i])
        for i in range(15)
    ]
    fw = [send(gathered.at[:, block, :], gathered.at[:, block, :], send_fw.at[15], recv_fw.at[15], pair)]

    for copy in edges:
        copy.wait_recv()
    for j in range(8):
        for q in range(4):
            at = 32 * j + 8 * q
            totals = []
            for p in range(3):
                t = [pltpu.roll(canvas[p, i, pl.ds(MARGIN + at, 8), :], 96, 1) for i in range(3)]
                left = jnp.where(lane8 < 96, t[0], t[1])
                right = jnp.where(lane8 < 96, t[1], t[2])
                if j in (0, 7):
                    side = 0 if j == 0 else 1
                    keep_v = has_n if j == 0 else has_s
                    band = from_ns[side, p, pl.ds(8 * q, 8), :]
                    left = left + jnp.where(keep_v, band[:, :128], zero8)
                    right = right + jnp.where(keep_v, band[:, 128:], zero8)
                    west = strip(from_corner, (2 * side, p, slice(0, 8)), q, 0, has_w & keep_v)
                    east = strip(from_corner, (2 * side + 1, p, slice(0, 8)), q, 96, has_e & keep_v)
                    left = left + jnp.where(first, west, zero8)
                    right = right + jnp.where(lane8 >= 96, east, zero8)
                west = strip(from_we, (0, p, pl.ds(8 * j, 8)), q, 0, has_w)
                east = strip(from_we, (1, p, pl.ds(8 * j, 8)), q, 96, has_e)
                left = left + jnp.where(first, west, zero8)
                right = right + jnp.where(lane8 >= 96, east, zero8)
                totals.append((left, right))
            for s in range(2):
                scale = 1.0 / (totals[2][s] + regular)
                for p in range(2):
                    here = (p, pl.ds(at, 8), slice(128 * s, 128 * s + 128))
                    out_obj[here] = obj[here] + totals[p][s] * scale

    for i in reversed(range(15)):
        x_, y_ = behind_plane[i]
        at = pl.ds(pl.multiple_of(HALF * core + 8 * (4 * x_ + y_), 8), 8)
        arrive(gathered.at[:, at, :], recv_ag.at[i])
        fw.append(send(gathered.at[:, at, :], gathered.at[:, at, :], send_fw.at[i], recv_fw.at[i], pair))
    for i in range(16):
        x_, y_ = behind_plane[i] if i < 15 else (x, y)
        at = pl.ds(pl.multiple_of(HALF * (1 - core) + 8 * (4 * x_ + y_), 8), 8)
        arrive(gathered.at[:, at, :], recv_fw.at[i])
    power = jnp.zeros((8, W), F32)
    for p in range(2):
        g = gathered[p]
        power = power + (g * g).reshape(32, 8, W).sum(axis=0)
    scale = jnp.sqrt(jnp.full((8, W), target, F32) / (jnp.sum(power) + epsilon))
    for p in range(2):
        out_probe[p] = gathered[p] * jnp.concatenate([scale] * 32, axis=0)

    for copy in halo + [e0, c0] + e1 + e2 + c1 + c2 + edges + g1 + fw:
        copy.wait_send()


def write_kernel(obj, probe, out_obj, out_probe, sems):
    copies = [
        pltpu.make_async_copy(obj, out_obj, sems.at[0]),
        pltpu.make_async_copy(probe, out_probe, sems.at[1]),
    ]
    for copy in copies:
        copy.start()
    for copy in copies:
        copy.wait()


def vmem(*shape, dtype=F32):
    return pltpu.VMEM(shape, dtype)


def per_device(rows, cols, object_field, probe, amplitudes, positions):
    in_vmem = pl.BlockSpec(memory_space=pltpu.VMEM)
    in_hbm = pl.BlockSpec(memory_space=pltpu.HBM)
    dma = pltpu.SemaphoreType.DMA
    results = pl.pallas_call(
        functools.partial(kernel, rows, cols),
        out_shape=(jax.ShapeDtypeStruct((2, W, W), F32),) * 2,
        in_specs=[in_hbm] * 6,
        out_specs=(in_vmem,) * 2,
        scratch_shapes=[
            pltpu.SMEM((1, 1, 2, FRAMES), jnp.int32),
            vmem(2, W, W),
            vmem(2, W, W),
            vmem(FRAMES, 2, W, 128),
            vmem(4, 2, W, W, dtype=BF16),
            vmem(W, W, dtype=BF16),
            vmem(2, 2, 64, 128),
            vmem(2, 2, 32, W),
            vmem(2, 2, 64, 128),
            vmem(4, 2, 8, 128),
            vmem(2, 3, SIDE, 128),
            vmem(FRAMES, 3, 3, LEAD + W + LEAD, 128),
            vmem(FRAMES, 2, W, W),
            vmem(FRAMES, W, W),
            vmem(FRAMES, 4, 2, 2, W, W, dtype=BF16),
            vmem(FRAMES, 4, 2, W, W),
            vmem(2, W, W),
            vmem(2 * W, 128),
            vmem(3, 3, SIDE, 128),
            vmem(2, 3, 80, 128),
            vmem(2, 3, 32, W),
            vmem(2, 3, 32, W),
            vmem(2, 3, 64, 128),
            vmem(4, 3, 8, 128),
            vmem(W + 8, 128),
            vmem(W + 8, 128),
            vmem(16, 24, 128),
            vmem(16, 24, 128),
            vmem(8, 24, 128),
            vmem(2, HALF, W),
            vmem(2, HALF, W),
            vmem(15, 2, 8, W),
            vmem(8, 2, 8, W),
            vmem(2, W, W),
            dma((5,)),
            dma((2 * FRAMES,)),
            dma((8,)),
            dma((8,)),
            dma((16,)),
            dma((16,)),
            dma((2,)),
            dma((2,)),
            dma((15,)),
            dma((16,)),
            dma((7,)),
            dma((8,)),
            dma((15,)),
            dma((15,)),
            dma((7,)),
            dma((8,)),
            dma((15,)),
            dma((15,)),
            dma((16,)),
            dma((16,)),
        ],
        compiler_params=pltpu.CompilerParams(
            collective_id=0, has_side_effects=True, vmem_limit_bytes=48 * 2**20
        ),
        name="ptycho",
    )(
        *(
            pltpu.with_memory_space_constraint(a, pltpu.HBM)
            for a in (
                jnp.swapaxes(positions, 2, 3),
                object_field,
                probe,
                amplitudes,
                jnp.asarray(dft_tables()),
                jnp.asarray(sort_table()),
            )
        ),
    )
    return pl.pallas_call(
        write_kernel,
        out_shape=(jax.ShapeDtypeStruct((2, W, W), F32),) * 2,
        in_specs=[in_vmem] * 2,
        out_specs=(in_hbm,) * 2,
        scratch_shapes=[dma((2,))],
        compiler_params=pltpu.CompilerParams(vmem_limit_bytes=2**20),
        name="write",
    )(*results)


def solution(mesh):
    return jax.shard_map(
        functools.partial(per_device, mesh.shape["row"], mesh.shape["col"]),
        mesh=mesh,
        in_specs=(
            P(None, "row", "col"),
            P(),
            P("row", "col", None, None, None),
            P("row", "col", None, None),
        ),
        out_specs=(P(None, "row", "col"), P()),
        check_vma=False,
    )
```

```python
import functools
import math

import jax
import jax.numpy as jnp
import numpy as np
from jax import lax
from jax.experimental import pallas as pl
from jax.experimental.pallas import tpu as pltpu
from jax.sharding import PartitionSpec as P

W = 256
HALF = W // 2
MARGIN = 32
FRAMES = 4
SIDE = W + 2 * MARGIN
LEAD = 2 * MARGIN

smoothing = 0.1
regular = 1.0
epsilon = 1e-06

MESH = pl.DeviceIdType.MESH
F32 = jnp.float32
BF16 = jnp.bfloat16

COMPASS = ((-1, 0), (1, 0), (0, -1), (0, 1), (-1, -1), (-1, 1), (1, -1), (1, 1))


def dft_tables():
    k = np.arange(HALF)
    j = np.arange(HALF)
    mats = []
    for parity in (0, 1):
        phase = (2 * k[:, None] + parity) * j[None, :] % W
        z = np.exp(-2j * np.pi * phase / W) / math.sqrt(W)
        mats.append(np.block([[z.real, -z.imag], [z.imag, z.real]]))
    mats += [m.T for m in mats]
    full = np.stack(mats)
    high = full.astype(BF16)
    low = (full - high.astype(np.float64)).astype(BF16)
    return np.stack([high, low], 1)


def sort_table():
    table = np.zeros((W, W), np.float32)
    k = np.arange(HALF)
    table[2 * k, k] = 1
    table[2 * k + 1, HALF + k] = 1
    return table.astype(BF16)


def split(x):
    high = x.astype(BF16)
    return high, (x - high.astype(F32)).astype(BF16)


def lanes(rows=8):
    return lax.broadcasted_iota(jnp.int32, (rows, 128), 1)


def neighbours(r, c, rows, cols):
    return [(lax.rem(r + dr + rows, rows), lax.rem(c + dc + cols, cols)) for dr, dc in COMPASS]


def pack(blocks, shift):
    group = lanes() // 32
    out = None
    for q, block in enumerate(blocks):
        amount = (shift + 32 * q) % 128
        turned = pltpu.roll(block, amount, 1) if amount else block
        out = turned if out is None else jnp.where(group == q, turned, out)
    return out


STEP = 16


def triple(left, right):
    a = jnp.concatenate([left[0], left[0], left[1]], axis=1)
    b = jnp.concatenate([right[0], right[1], right[0]], axis=0)
    return jnp.dot(a, b, preferred_element_type=F32)


def send(src, dst, sends, recvs, device):
    copy = pltpu.make_async_remote_copy(
        src_ref=src, dst_ref=dst, send_sem=sends, recv_sem=recvs, device_id=device, device_id_type=MESH
    )
    copy.start()
    return copy


def kernel(
    rows,
    cols,
    pos_hbm,
    obj_hbm,
    probe_hbm,
    amps_hbm,
    table_hbm,
    sort_hbm,
    out_obj,
    out_probe,
    pos,
    obj,
    probe,
    amps,
    table,
    sort,
    halo_strips,
    halo_ns,
    halo_we,
    halo_corner,
    ext,
    spread,
    win,
    wave,
    sorted_amp,
    half,
    mid,
    acc,
    power2,
    canvas,
    strips,
    bands,
    from_ns,
    from_we,
    from_corner,
    early0,
    early0_got,
    early1,
    early1_got,
    early2,
    got0,
    part0,
    got1,
    all2,
    gathered,
    load_sem,
    amp_sem,
    send_halo,
    recv_halo,
    send_edge,
    recv_edge,
    send_pair,
    recv_pair,
    send_e1,
    recv_e1,
    send_e2,
    recv_e2,
    send_m1,
    recv_m1,
    send_m2,
    recv_m2,
    send_ag,
    recv_ag,
    send_fw,
    recv_fw,
):
    loads = [
        pltpu.make_async_copy(src, dst, load_sem.at[i])
        for i, (src, dst) in enumerate(
            ((obj_hbm, obj), (probe_hbm, probe), (sort_hbm, sort), (table_hbm, table), (pos_hbm, pos))
        )
    ]
    loads[0].start()
    amp_loads = []
    for f in range(FRAMES):
        for t in range(2):
            amp_loads.append(
                pltpu.make_async_copy(
                    amps_hbm.at[0, 0, f, :, 128 * t : 128 * t + 128], amps.at[f, t], amp_sem
                )
            )

    r, c = lax.axis_index("row"), lax.axis_index("col")
    core, x, y_lo = lax.rem(c, 2), lax.rem(c // 2, 4), c // 8
    y_hi, z = lax.rem(r, 2), r // 2
    y = 2 * y_hi + y_lo

    def place(core_, x_, y_, z_):
        return (2 * z_ + y_ // 2, (lax.rem(y_, 2) * 4 + x_) * 2 + core_)

    around = neighbours(r, c, rows, cols)
    pair = place(1 - core, x, y, z)
    steps_xy = [(2, 2), (1, 2), (3, 2), (2, 1), (2, 3), (1, 1), (1, 3), (3, 1), (3, 3), (2, 0), (0, 2), (1, 0), (3, 0), (0, 1), (0, 3)]
    far = [min(dx, 4 - dx) + min(dy, 4 - dy) - 1 for dx, dy in steps_xy]
    on_plane = [(lax.rem(x + dx, 4), lax.rem(y + dy, 4)) for dx, dy in steps_xy]
    behind_plane = [(lax.rem(x + 4 - dx, 4), lax.rem(y + 4 - dy, 4)) for dx, dy in steps_xy]
    plane = [place(core, x_, y_, z) for x_, y_ in on_plane]
    steps_z = [4, 3, 5, 2, 6, 1, 7]
    column = [place(core, x, y, lax.rem(z + d, 8)) for d in steps_z]
    everyone = column[:1] + plane[:1] + around[4:] + column[1:3] + plane[1:5] + around[:4] + plane[5:] + column[3:] + [pair]
    barrier = pltpu.get_barrier_semaphore()
    for partner in everyone:
        pl.semaphore_signal(barrier, inc=1, device_id=partner, device_id_type=MESH)
    loads[1].start()
    loads[4].start()
    loads[2].start()
    for load in amp_loads:
        load.start()
    loads[3].start()

    def arrive(dst, recvs):
        pltpu.make_async_remote_copy(
            src_ref=dst, dst_ref=dst, send_sem=recvs, recv_sem=recvs, device_id=pair, device_id_type=MESH
        ).wait_recv()

    def sent(src, sends):
        pltpu.make_async_remote_copy(
            src_ref=src, dst_ref=src, send_sem=sends, recv_sem=sends, device_id=pair, device_id_type=MESH
        ).wait_send()

    def room(count):
        return mid.at[0, 0, 0 : count // W, :]

    loads[0].wait()
    for p in range(2):
        for j in range(8):
            left = [obj[p, pl.ds(32 * j + 8 * q, 8), 0:128] for q in range(4)]
            right = [obj[p, pl.ds(32 * j + 8 * q, 8), 128:256] for q in range(4)]
            halo_strips[0, p, pl.ds(8 * j, 8), :] = pack(left, 0)
            halo_strips[1, p, pl.ds(8 * j, 8), :] = pack(right, 32)
    pl.semaphore_wait(barrier, len(everyone))
    moves = (
        (obj.at[:, 0:32, :], halo_ns.at[1]),
        (obj.at[:, W - 32 : W, :], halo_ns.at[0]),
        (halo_strips.at[0], halo_we.at[1]),
        (halo_strips.at[1], halo_we.at[0]),
        (halo_strips.at[0, :, 0:8, :], halo_corner.at[3]),
        (halo_strips.at[1, :, 0:8, :], halo_corner.at[2]),
        (halo_strips.at[0, :, 56:64, :], halo_corner.at[1]),
        (halo_strips.at[1, :, 56:64, :], halo_corner.at[0]),
    )
    for i in (4, 5, 6, 7, 0, 1, 2, 3):
        send(moves[i][0], moves[i][1], send_halo, recv_halo.at[int(i in (2, 3))], around[i])

    lane = lanes(STEP)
    zero = jnp.zeros((STEP, 128), F32)

    def clear(i, _):
        for f in range(FRAMES):
            for p in range(3):
                for t in range(3):
                    spread[f, p, t, pl.ds(16 * i, 16), :] = zero
                    spread[f, p, t, pl.ds(LEAD + W + 16 * i, 16), :] = zero
        return 0

    lax.fori_loop(0, LEAD // 16, clear, 0)
    loads[1].wait()
    loads[4].wait()
    loads[2].wait()
    pltpu.make_async_copy(amps, amps, amp_sem).wait()
    sums = jnp.zeros((8, 128), F32)
    for f in range(FRAMES):
        parts = []
        for parity in (0, 1):
            a = jnp.concatenate([amps[f, t, pl.ds(parity, HALF, stride=2), :] for t in range(2)], axis=1)
            squares = a * a
            sums = sums + (squares[:, :128] + squares[:, 128:]).reshape(16, 8, 128).sum(axis=0)
            high = a.astype(BF16)
            rest = a - high.astype(F32)
            middle = rest.astype(BF16)
            low = (rest - middle.astype(F32)).astype(BF16)
            parts.append(jnp.concatenate([high, middle, low], axis=1))
        both = jnp.concatenate(parts, axis=0)
        sorter = sort[...]
        sorted_amp[f] = jnp.dot(
            both, jnp.concatenate([sorter, sorter, sorter], axis=0), preferred_element_type=F32
        )
    early0[pl.ds(W, 8), :] = sums

    at_row = [pos[0, 0, 0, f] for f in range(FRAMES)]
    at_col = [pos[0, 0, 1, f] for f in range(FRAMES)]

    def gather(f, p, row):
        b = at_col[f]
        tiles = [ext[p, t, pl.ds(at_row[f] + row, STEP), :] for t in range(3)]
        turned = [pltpu.roll(t, lax.rem(128 - b, 128), 1) for t in tiles]
        keep = lane < 128 - b
        return jnp.concatenate(
            [jnp.where(keep, turned[0], turned[1]), jnp.where(keep, turned[1], turned[2])], axis=1
        )

    def scatter(f, p, row, value):
        b = at_col[f]
        behind = lane >= b
        v0, v1 = pltpu.roll(value[:, :128], b, 1), pltpu.roll(value[:, 128:], b, 1)
        at = pl.ds(LEAD + row, STEP)
        spread[f, p, 0, at, :] = jnp.where(behind, v0, zero)
        spread[f, p, 1, at, :] = jnp.where(behind, v1, v0)
        spread[f, p, 2, at, :] = jnp.where(behind, zero, v1)

    for row in range(0, W, STEP):
        here = pl.ds(row, STEP)
        pr, pi = probe[0, here, :], probe[1, here, :]
        for f in range(FRAMES):
            scatter(f, 2, row, pr * pr + pi * pi)

    def gather_canvas(planes):
        def some(i, _):
            row = pl.multiple_of(16 * i, 16)
            for p in planes:
                for t in range(3):
                    total = spread[0, p, t, pl.ds(LEAD - at_row[0] + row, 16), :]
                    for f in range(1, FRAMES):
                        total = total + spread[f, p, t, pl.ds(LEAD - at_row[f] + row, 16), :]
                    canvas[p, t, pl.ds(row, 16), :] = total
            return 0

        lax.fori_loop(0, SIDE // 16, some, 0)

    lane8 = lanes()
    first = lane8 < 32
    second = lane8 < 64
    zero8 = jnp.zeros((8, 128), F32)
    has_n, has_s = r > 0, r < rows - 1
    has_w, has_e = c > 0, c < cols - 1

    def strip(ref, at, q, target, keep):
        amount = (target - 32 * q) % 128
        block = ref[at]
        block = pltpu.roll(block, amount, 1) if amount else block
        return jnp.where(keep, block, zero8)

    def pack_edges(planes):
        for p in planes:
            for side, base in enumerate((0, MARGIN + W)):
                for q in range(4):
                    t = [pltpu.roll(canvas[p, i, pl.ds(base + 8 * q, 8), :], 96, 1) for i in range(3)]
                    bands[side, p, pl.ds(8 * q, 8), 0:128] = jnp.where(lane8 < 96, t[0], t[1])
                    bands[side, p, pl.ds(8 * q, 8), 128:256] = jnp.where(lane8 < 96, t[1], t[2])
            for j in range(10):
                left = [canvas[p, 0, pl.ds(32 * j + 8 * q, 8), :] for q in range(4)]
                right = [canvas[p, 2, pl.ds(32 * j + 8 * q, 8), :] for q in range(4)]
                strips[0, p, pl.ds(8 * j, 8), :] = pack(left, 0)
                strips[1, p, pl.ds(8 * j, 8), :] = pack(right, 96)

    def send_edges(planes):
        at = pl.ds(planes[0], len(planes))
        moves = (
            (bands.at[0, at], from_ns.at[1, at]),
            (bands.at[1, at], from_ns.at[0, at]),
            (strips.at[0, at, 8:72, :], from_we.at[1, at]),
            (strips.at[1, at, 8:72, :], from_we.at[0, at]),
            (strips.at[0, at, 0:8, :], from_corner.at[3, at]),
            (strips.at[1, at, 0:8, :], from_corner.at[2, at]),
            (strips.at[0, at, 72:80, :], from_corner.at[1, at]),
            (strips.at[1, at, 72:80, :], from_corner.at[0, at]),
        )
        for i in (4, 5, 6, 7, 0, 1, 2, 3):
            send(moves[i][0], moves[i][1], send_edge, recv_edge, around[i])

    gather_canvas((2,))
    pack_edges((2,))
    loads[3].wait()

    def put(p, row, centre, west, east):
        t0, t1 = pltpu.roll(centre[0], 32, 1), pltpu.roll(centre[1], 32, 1)
        ext[p, 0, pl.ds(row, 8), :] = jnp.where(first, west, t0)
        ext[p, 1, pl.ds(row, 8), :] = jnp.where(first, t0, t1)
        ext[p, 2, pl.ds(row, 8), :] = jnp.where(first, t1, jnp.where(second, east, zero8))

    arrive(room(2 * 2 * 64 * 128), recv_halo.at[1])
    for p in range(2):
        for j in range(8):
            for q in range(4):
                at = 32 * j + 8 * q
                block = obj[p, pl.ds(at, 8), :]
                west = strip(halo_we, (0, p, pl.ds(8 * j, 8)), q, 0, has_w)
                east = strip(halo_we, (1, p, pl.ds(8 * j, 8)), q, 32, has_e)
                put(p, MARGIN + at, (block[:, :128], block[:, 128:]), west, east)
    def halve(f, stage, side, rows_at, value):
        h, l = split(value)
        half[stage, side, 0, pl.ds(W * f + rows_at.start, rows_at.size), :] = h
        half[stage, side, 1, pl.ds(W * f + rows_at.start, rows_at.size), :] = l

    def first_step(some_rows):
        for row in some_rows:
            sums = [jnp.zeros((STEP, W), F32)] * 2
            for f in range(FRAMES):
                waves = []
                for i, base in enumerate((row, HALF + row)):
                    here = pl.ds(base, STEP)
                    wr, wi = gather(f, 0, base), gather(f, 1, base)
                    pr, pi = probe[0, here, :], probe[1, here, :]
                    win[f, 0, here, :] = wr
                    win[f, 1, here, :] = wi
                    sums[i] = sums[i] + (wr * wr + wi * wi)
                    waves.append((pr * wr - pi * wi, pr * wi + pi * wr))
                    wave[f, 0, here, :], wave[f, 1, here, :] = waves[-1]
                for part in range(2):
                    top, low = waves[0][part], waves[1][part]
                    where = pl.ds(HALF * part + row, STEP)
                    halve(f, 0, 0, where, top + low)
                    halve(f, 0, 1, where, top - low)
            for i, base in enumerate((row, HALF + row)):
                power2[pl.ds(base, STEP), :] = sums[i][:, :128]
                power2[pl.ds(W + base, STEP), :] = sums[i][:, 128:]

    first_step(range(MARGIN, HALF - MARGIN, STEP))
    arrive(room(2 * 2 * 32 * W + 4 * 2 * 8 * 128), recv_halo.at[0])
    for p in range(2):
        for k in range(4):
            for side, (keep_v, base) in enumerate(((has_n, 0), (has_s, MARGIN + W))):
                block = halo_ns[side, p, pl.ds(8 * k, 8), :]
                block = jnp.where(keep_v, block, jnp.zeros_like(block))
                west = strip(halo_corner, (2 * side, p, slice(0, 8)), k, 0, has_w & keep_v)
                east = strip(halo_corner, (2 * side + 1, p, slice(0, 8)), k, 32, has_e & keep_v)
                put(p, base + 8 * k, (block[:, :128], block[:, 128:]), west, east)

    send_edges((2,))
    first_step([*range(0, MARGIN, STEP), *range(HALF - MARGIN, HALF, STEP)])

    mine8 = pl.multiple_of(core * HALF, HALF)
    other8 = pl.multiple_of((1 - core) * HALF, HALF)
    for t in range(2):
        early0[pl.ds(HALF * t, HALF), :] = power2[pl.ds(W * t + other8, HALF), :]
    e0 = send(early0, early0_got, send_pair.at[0], recv_pair.at[0], pair)

    def left_dots(stage, flip):
        for f in range(FRAMES):
            here = pl.ds(W * f, W)
            for side in range(2):
                mid[stage, side, here, :] = triple(
                    (table[flip + side, 0], table[flip + side, 1]),
                    (half[stage, side, 0, here, :], half[stage, side, 1, here, :]),
                )

    def right_dots(stage, flip):
        for side in range(2):
            mid[stage, side] = triple(
                (half[stage, side, 0], half[stage, side, 1]),
                (table[flip + side, 0], table[flip + side, 1]),
            )

    left_dots(0, 0)
    for f in range(FRAMES):
        for parity in range(2):
            for row in range(0, HALF, STEP):
                zr = mid[0, parity, pl.ds(W * f + row, STEP), :]
                zi = mid[0, parity, pl.ds(W * f + HALF + row, STEP), :]
                here = pl.ds(HALF * parity + row, STEP)
                plus = jnp.concatenate([zr[:, :128] + zr[:, 128:], zi[:, :128] + zi[:, 128:]], axis=1)
                less = jnp.concatenate([zr[:, :128] - zr[:, 128:], zi[:, :128] - zi[:, 128:]], axis=1)
                halve(f, 1, 0, here, plus)
                halve(f, 1, 1, here, less)

    k = 4 * x + y
    e0.wait_recv()
    for i in range(16):
        for t in range(2):
            at = mine8 + 8 * i
            early1[i, pl.ds(8 * t, 8), :] = (
                power2[pl.ds(W * t + at, 8), :] + early0_got[pl.ds(HALF * t + 8 * i, 8), :]
            )
        early1[i, pl.ds(16, 8), :] = early0[pl.ds(W, 8), :] + early0_got[pl.ds(W, 8), :]
    early1_got[k] = early1[k]
    e1 = []
    for i, (x_, y_) in enumerate(on_plane):
        e1.append(send(early1.at[4 * x_ + y_], early1_got.at[k], send_e1.at[0], recv_e1.at[0], plane[i]))

    right_dots(1, 2)
    for f in range(FRAMES):
        for side in range(2):
            for row in range(0, W, STEP):
                here = pl.ds(row, STEP)
                amp = sorted_amp[f, here, 128 * side : 128 * side + 128]
                v = mid[1, side, pl.ds(W * f + row, STEP), :]
                zr, zi = v[:, :128], v[:, 128:]
                factor = amp * lax.rsqrt(zr * zr + zi * zi + smoothing)
                halve(f, 2, side, here, jnp.concatenate([zr * factor, zi * factor], axis=1))

    right_dots(2, 0)

    for f in range(FRAMES):
        for parity in range(2):
            for row in range(0, HALF, STEP):
                even, odd = (mid[2, i, pl.ds(W * f + HALF * parity + row, STEP), :] for i in range(2))
                plus, less = even + odd, even - odd
                for part in range(2):
                    cut = slice(128 * part, 128 * part + 128)
                    value = jnp.concatenate([plus[:, cut], less[:, cut]], axis=1)
                    halve(f, 3, parity, pl.ds(HALF * part + row, STEP), value)

    left_dots(3, 2)
    for row in range(0, HALF, STEP):
        parts = []
        for f in range(FRAMES):
            er, orr = (mid[3, i, pl.ds(W * f + row, STEP), :] for i in range(2))
            ei, oi = (mid[3, i, pl.ds(W * f + HALF + row, STEP), :] for i in range(2))
            parts.append(((er + orr, ei + oi), (er - orr, ei - oi)))
        for side, base in enumerate((row, HALF + row)):
            here = pl.ds(base, STEP)
            pr, pi = probe[0, here, :], probe[1, here, :]
            sums = [jnp.zeros((STEP, W), F32)] * 2
            for f in range(FRAMES):
                wr, wi = win[f, 0, here, :], win[f, 1, here, :]
                dr = parts[f][side][0] - wave[f, 0, here, :]
                di = parts[f][side][1] - wave[f, 1, here, :]
                scatter(f, 0, base, pr * dr + pi * di)
                scatter(f, 1, base, pr * di - pi * dr)
                sums = [sums[0] + (wr * dr + wi * di), sums[1] + (wr * di - wi * dr)]
            acc[0, here, :], acc[1, here, :] = sums

    mine = pl.ds(mine8, HALF)
    other = pl.ds(other8, HALF)
    c0 = [
        send(acc.at[p, other, :], got0.at[p], send_pair.at[1 + p], recv_pair.at[1 + p], pair) for p in range(2)
    ]

    gather_canvas((0, 1))

    c1 = []
    for p in range(2):
        c0[p].wait_recv()
        part0[p] = acc[p, mine, :] + got0[p]
        for i, (x_, y_) in enumerate(on_plane):
            src = part0.at[p, pl.ds(pl.multiple_of(8 * (4 * x_ + y_), 8), 8), :]
            c1.append(send(src, got1.at[p, i], send_m1.at[p], recv_m1.at[p], plane[i]))

    pack_edges((0, 1))
    arrive(early1_got.at[0:15], recv_e1.at[0])
    total = early1_got[0]
    for i in range(1, 16):
        total = total + early1_got[i]
    early2[z] = total
    e2 = [send(early2.at[z], early2.at[z], send_e2.at[0], recv_e2.at[0], column[i]) for i in range(7)]

    own = pl.ds(pl.multiple_of(8 * k, 8), 8)
    c2 = []
    for p in range(2):
        arrive(got1.at[p], recv_m1.at[p])
        total = part0[p, own, :]
        for i in range(15):
            total = total + got1[p, i]
        all2[p, z] = total
        for i in range(7):
            c2.append(
                send(all2.at[p, z], all2.at[p, z], send_m2.at[p], recv_m2.at[p], column[i])
            )

    send_edges((0, 1))

    arrive(early2.at[0:7], recv_e2.at[0])
    total = early2[0]
    for i in range(1, 8):
        total = total + early2[i]
    weight = 1.0 / (jnp.concatenate([total[0:8], total[8:16]], axis=1) + regular)
    target = jnp.sum(total[16:24]) * (1.0 / (FRAMES * rows * cols))

    block = pl.ds(pl.multiple_of(HALF * core + 8 * k, 8), 8)
    for p in range(2):
        arrive(all2.at[p, 0:7], recv_m2.at[p])
        total = all2[p, 0]
        for i in range(1, 8):
            total = total + all2[p, i]
        gathered[p, block, :] = probe[p, block, :] + total * weight
        here = gathered.at[p, block, :]
        for i in range(15):
            send(here, here, send_ag.at[p], recv_ag.at[4 * p + far[i]], plane[i])
        send(here, here, send_fw.at[p], recv_fw.at[p], pair)

    for p in range(2):
        for distance in range(4):
            batch = [i for i in range(15) if far[i] == distance]
            arrive(gathered.at[p, 0 : 8 * len(batch)], recv_ag.at[4 * p + distance])
            for i in batch:
                x_, y_ = behind_plane[i]
                here = gathered.at[p, pl.ds(pl.multiple_of(HALF * core + 8 * (4 * x_ + y_), 8), 8), :]
                send(here, here, send_fw.at[p], recv_fw.at[p], pair)
    arrive(room(3 * (2 * 32 * W + 2 * 64 * 128 + 4 * 8 * 128)), recv_edge)
    for j in range(8):
        for q in range(4):
            at = 32 * j + 8 * q
            totals = []
            for p in range(3):
                t = [pltpu.roll(canvas[p, i, pl.ds(MARGIN + at, 8), :], 96, 1) for i in range(3)]
                left = jnp.where(lane8 < 96, t[0], t[1])
                right = jnp.where(lane8 < 96, t[1], t[2])
                if j in (0, 7):
                    side = 0 if j == 0 else 1
                    keep_v = has_n if j == 0 else has_s
                    band = from_ns[side, p, pl.ds(8 * q, 8), :]
                    left = left + jnp.where(keep_v, band[:, :128], zero8)
                    right = right + jnp.where(keep_v, band[:, 128:], zero8)
                    west = strip(from_corner, (2 * side, p, slice(0, 8)), q, 0, has_w & keep_v)
                    east = strip(from_corner, (2 * side + 1, p, slice(0, 8)), q, 96, has_e & keep_v)
                    left = left + jnp.where(first, west, zero8)
                    right = right + jnp.where(lane8 >= 96, east, zero8)
                west = strip(from_we, (0, p, pl.ds(8 * j, 8)), q, 0, has_w)
                east = strip(from_we, (1, p, pl.ds(8 * j, 8)), q, 96, has_e)
                left = left + jnp.where(first, west, zero8)
                right = right + jnp.where(lane8 >= 96, east, zero8)
                totals.append((left, right))
            for s in range(2):
                scale = 1.0 / (totals[2][s] + regular)
                for p in range(2):
                    here = (p, pl.ds(at, 8), slice(128 * s, 128 * s + 128))
                    out_obj[here] = obj[here] + totals[p][s] * scale

    for copy in [e0] + c0:
        copy.wait_send()
    sent(room(2 * (2 * 32 * W + 2 * 64 * 128 + 4 * 8 * 128)), send_halo)
    sent(room(3 * (2 * 32 * W + 2 * 64 * 128 + 4 * 8 * 128)), send_edge)
    sent(early1.at[0:15], send_e1.at[0])
    sent(early2.at[0:7], send_e2.at[0])
    for p in range(2):
        sent(got1.at[p], send_m1.at[p])
        sent(all2.at[p, 0:7], send_m2.at[p])

    for p in range(2):
        arrive(gathered.at[p, other, :], recv_fw.at[p])
    power = jnp.zeros((8, W), F32)
    for p in range(2):
        g = gathered[p]
        power = power + (g * g).reshape(32, 8, W).sum(axis=0)
    scale = jnp.sqrt(jnp.full((8, W), target, F32) / (jnp.sum(power) + epsilon))
    for p in range(2):
        out_probe[p] = gathered[p] * jnp.concatenate([scale] * 32, axis=0)

    for p in range(2):
        sent(gathered.at[p, 0:120], send_ag.at[p])
        sent(gathered.at[p, mine, :], send_fw.at[p])


def write_kernel(obj, probe, out_obj, out_probe, sems):
    copies = [
        pltpu.make_async_copy(obj, out_obj, sems.at[0]),
        pltpu.make_async_copy(probe, out_probe, sems.at[1]),
    ]
    for copy in copies:
        copy.start()
    for copy in copies:
        copy.wait()


def vmem(*shape, dtype=F32):
    return pltpu.VMEM(shape, dtype)


def per_device(rows, cols, object_field, probe, amplitudes, positions):
    in_vmem = pl.BlockSpec(memory_space=pltpu.VMEM)
    in_hbm = pl.BlockSpec(memory_space=pltpu.HBM)
    dma = pltpu.SemaphoreType.DMA
    results = pl.pallas_call(
        functools.partial(kernel, rows, cols),
        out_shape=(jax.ShapeDtypeStruct((2, W, W), F32),) * 2,
        in_specs=[in_hbm] * 6,
        out_specs=(in_vmem,) * 2,
        scratch_shapes=[
            pltpu.SMEM((1, 1, 2, FRAMES), jnp.int32),
            vmem(2, W, W),
            vmem(2, W, W),
            vmem(FRAMES, 2, W, 128),
            vmem(4, 2, W, W, dtype=BF16),
            vmem(W, W, dtype=BF16),
            vmem(2, 2, 64, 128),
            vmem(2, 2, 32, W),
            vmem(2, 2, 64, 128),
            vmem(4, 2, 8, 128),
            vmem(2, 3, SIDE, 128),
            vmem(FRAMES, 3, 3, LEAD + W + LEAD, 128),
            vmem(FRAMES, 2, W, W),
            vmem(FRAMES, 2, W, W),
            vmem(FRAMES, W, W),
            vmem(4, 2, 2, FRAMES * W, W, dtype=BF16),
            vmem(4, 2, FRAMES * W, W),
            vmem(2, W, W),
            vmem(2 * W, 128),
            vmem(3, 3, SIDE, 128),
            vmem(2, 3, 80, 128),
            vmem(2, 3, 32, W),
            vmem(2, 3, 32, W),
            vmem(2, 3, 64, 128),
            vmem(4, 3, 8, 128),
            vmem(W + 8, 128),
            vmem(W + 8, 128),
            vmem(16, 24, 128),
            vmem(16, 24, 128),
            vmem(8, 24, 128),
            vmem(2, HALF, W),
            vmem(2, HALF, W),
            vmem(2, 15, 8, W),
            vmem(2, 8, 8, W),
            vmem(2, W, W),
            dma((5,)),
            dma,
            dma,
            dma((2,)),
            dma,
            dma,
            dma((3,)),
            dma((3,)),
            dma((1,)),
            dma((1,)),
            dma((1,)),
            dma((1,)),
            dma((2,)),
            dma((2,)),
            dma((2,)),
            dma((2,)),
            dma((2,)),
            dma((8,)),
            dma((2,)),
            dma((2,)),
        ],
        compiler_params=pltpu.CompilerParams(
            collective_id=0, has_side_effects=True, vmem_limit_bytes=48 * 2**20
        ),
        name="ptycho",
    )(
        *(
            pltpu.with_memory_space_constraint(a, pltpu.HBM)
            for a in (
                jnp.swapaxes(positions, 2, 3),
                object_field,
                probe,
                amplitudes,
                jnp.asarray(dft_tables()),
                jnp.asarray(sort_table()),
            )
        ),
    )
    return pl.pallas_call(
        write_kernel,
        out_shape=(jax.ShapeDtypeStruct((2, W, W), F32),) * 2,
        in_specs=[in_vmem] * 2,
        out_specs=(in_hbm,) * 2,
        scratch_shapes=[dma((2,))],
        compiler_params=pltpu.CompilerParams(vmem_limit_bytes=2**20),
        name="write",
    )(*results)


def solution(mesh):
    return jax.shard_map(
        functools.partial(per_device, mesh.shape["row"], mesh.shape["col"]),
        mesh=mesh,
        in_specs=(
            P(None, "row", "col"),
            P(),
            P("row", "col", None, None, None),
            P("row", "col", None, None),
        ),
        out_specs=(P(None, "row", "col"), P()),
        check_vma=False,
    )
```

```python
import functools
import math

import jax
import jax.numpy as jnp
import numpy as np
from jax import lax
from jax.experimental import pallas as pl
from jax.experimental.pallas import tpu as pltpu
from jax.sharding import PartitionSpec as P

W = 256
HALF = W // 2
MARGIN = 32
FRAMES = 4
SIDE = W + 2 * MARGIN
LEAD = 2 * MARGIN

smoothing = 0.1
regular = 1.0
epsilon = 1e-06

MESH = pl.DeviceIdType.MESH
F32 = jnp.float32
BF16 = jnp.bfloat16

COMPASS = ((-1, 0), (1, 0), (0, -1), (0, 1), (-1, -1), (-1, 1), (1, -1), (1, 1))


def dft_tables():
    k = np.arange(HALF)
    j = np.arange(HALF)
    mats = []
    for parity in (0, 1):
        phase = (2 * k[:, None] + parity) * j[None, :] % W
        z = np.exp(-2j * np.pi * phase / W) / math.sqrt(W)
        mats.append(np.block([[z.real, -z.imag], [z.imag, z.real]]))
    mats += [m.T for m in mats]
    full = np.stack(mats)
    high = full.astype(BF16)
    low = (full - high.astype(np.float64)).astype(BF16)
    return np.stack([high, low], 1)


def sort_table():
    table = np.zeros((W, W), np.float32)
    k = np.arange(HALF)
    table[2 * k, k] = 1
    table[2 * k + 1, HALF + k] = 1
    return table.astype(BF16)


def split(x):
    high = x.astype(BF16)
    return high, (x - high.astype(F32)).astype(BF16)


def lanes(rows=8):
    return lax.broadcasted_iota(jnp.int32, (rows, 128), 1)


def neighbours(r, c, rows, cols):
    return [(lax.rem(r + dr + rows, rows), lax.rem(c + dc + cols, cols)) for dr, dc in COMPASS]


def pack(blocks, shift):
    group = lanes() // 32
    out = None
    for q, block in enumerate(blocks):
        amount = (shift + 32 * q) % 128
        turned = pltpu.roll(block, amount, 1) if amount else block
        out = turned if out is None else jnp.where(group == q, turned, out)
    return out


STEP = 16


def triple(left, right):
    a = jnp.concatenate([left[0], left[0], left[1]], axis=1)
    b = jnp.concatenate([right[0], right[1], right[0]], axis=0)
    return jnp.dot(a, b, preferred_element_type=F32)


def send(src, dst, sends, recvs, device):
    copy = pltpu.make_async_remote_copy(
        src_ref=src, dst_ref=dst, send_sem=sends, recv_sem=recvs, device_id=device, device_id_type=MESH
    )
    copy.start()
    return copy


def kernel(
    rows,
    cols,
    pos_hbm,
    obj_hbm,
    probe_hbm,
    amps_hbm,
    table_hbm,
    sort_hbm,
    out_obj,
    out_probe,
    pos,
    obj,
    probe,
    amps,
    table,
    sort,
    halo_strips,
    halo_ns,
    halo_we,
    halo_corner,
    ext,
    spread,
    win,
    wave,
    sorted_amp,
    half,
    mid,
    acc,
    power2,
    canvas,
    strips,
    bands,
    from_ns,
    from_we,
    from_corner,
    early0,
    early0_got,
    early1,
    early1_got,
    early2,
    got0,
    part0,
    got1,
    all2,
    gathered,
    load_sem,
    amp_sem,
    send_halo,
    recv_halo,
    send_edge,
    recv_edge,
    send_pair,
    recv_pair,
    send_e1,
    recv_e1,
    send_e2,
    recv_e2,
    send_m1,
    recv_m1,
    send_m2,
    recv_m2,
    send_ag,
    recv_ag,
    send_fw,
    recv_fw,
):
    loads = [
        pltpu.make_async_copy(src, dst, load_sem.at[i])
        for i, (src, dst) in enumerate(
            ((obj_hbm, obj), (probe_hbm, probe), (sort_hbm, sort), (table_hbm, table), (pos_hbm, pos))
        )
    ]
    loads[0].start()
    amp_loads = []
    for f in range(FRAMES):
        for t in range(2):
            amp_loads.append(
                pltpu.make_async_copy(
                    amps_hbm.at[0, 0, f, :, 128 * t : 128 * t + 128], amps.at[f, t], amp_sem
                )
            )

    r, c = lax.axis_index("row"), lax.axis_index("col")
    core, x, y_lo = lax.rem(c, 2), lax.rem(c // 2, 4), c // 8
    y_hi, z = lax.rem(r, 2), r // 2
    y = 2 * y_hi + y_lo

    def place(core_, x_, y_, z_):
        return (2 * z_ + y_ // 2, (lax.rem(y_, 2) * 4 + x_) * 2 + core_)

    around = neighbours(r, c, rows, cols)
    pair = place(1 - core, x, y, z)
    steps_xy = [(2, 2), (1, 2), (3, 2), (2, 1), (2, 3), (1, 1), (1, 3), (3, 1), (3, 3), (2, 0), (0, 2), (1, 0), (3, 0), (0, 1), (0, 3)]
    far = [min(dx, 4 - dx) + min(dy, 4 - dy) - 1 for dx, dy in steps_xy]
    on_plane = [(lax.rem(x + dx, 4), lax.rem(y + dy, 4)) for dx, dy in steps_xy]
    behind_plane = [(lax.rem(x + 4 - dx, 4), lax.rem(y + 4 - dy, 4)) for dx, dy in steps_xy]
    plane = [place(core, x_, y_, z) for x_, y_ in on_plane]
    steps_z = [4, 3, 5, 2, 6, 1, 7]
    column = [place(core, x, y, lax.rem(z + d, 8)) for d in steps_z]
    everyone = column[:1] + plane[:1] + around[4:] + column[1:3] + plane[1:5] + around[:4] + plane[5:] + column[3:] + [pair]
    barrier = pltpu.get_barrier_semaphore()
    for partner in everyone:
        pl.semaphore_signal(barrier, inc=1, device_id=partner, device_id_type=MESH)
    loads[1].start()
    loads[4].start()
    loads[2].start()
    for load in amp_loads:
        load.start()
    loads[3].start()

    def arrive(dst, recvs):
        pltpu.make_async_remote_copy(
            src_ref=dst, dst_ref=dst, send_sem=recvs, recv_sem=recvs, device_id=pair, device_id_type=MESH
        ).wait_recv()

    def sent(src, sends):
        pltpu.make_async_remote_copy(
            src_ref=src, dst_ref=src, send_sem=sends, recv_sem=sends, device_id=pair, device_id_type=MESH
        ).wait_send()

    def room(count):
        return mid.at[0, 0, 0 : count // W, :]

    loads[0].wait()
    for p in range(2):
        for j in range(8):
            left = [obj[p, pl.ds(32 * j + 8 * q, 8), 0:128] for q in range(4)]
            right = [obj[p, pl.ds(32 * j + 8 * q, 8), 128:256] for q in range(4)]
            halo_strips[0, p, pl.ds(8 * j, 8), :] = pack(left, 0)
            halo_strips[1, p, pl.ds(8 * j, 8), :] = pack(right, 32)
    pl.semaphore_wait(barrier, len(everyone))
    moves = (
        (obj.at[:, 0:32, :], halo_ns.at[1]),
        (obj.at[:, W - 32 : W, :], halo_ns.at[0]),
        (halo_strips.at[0], halo_we.at[1]),
        (halo_strips.at[1], halo_we.at[0]),
        (halo_strips.at[0, :, 0:8, :], halo_corner.at[3]),
        (halo_strips.at[1, :, 0:8, :], halo_corner.at[2]),
        (halo_strips.at[0, :, 56:64, :], halo_corner.at[1]),
        (halo_strips.at[1, :, 56:64, :], halo_corner.at[0]),
    )
    for i in (4, 5, 6, 7, 0, 1, 2, 3):
        send(moves[i][0], moves[i][1], send_halo, recv_halo.at[int(i in (2, 3))], around[i])

    lane = lanes(STEP)
    zero = jnp.zeros((STEP, 128), F32)

    def clear(i, _):
        for f in range(FRAMES):
            for p in range(3):
                for t in range(3):
                    spread[f, p, t, pl.ds(16 * i, 16), :] = zero
                    spread[f, p, t, pl.ds(LEAD + W + 16 * i, 16), :] = zero
        return 0

    lax.fori_loop(0, LEAD // 16, clear, 0)
    loads[1].wait()
    loads[4].wait()
    loads[2].wait()
    pltpu.make_async_copy(amps, amps, amp_sem).wait()
    sums = jnp.zeros((8, 128), F32)
    for f in range(FRAMES):
        parts = []
        for parity in (0, 1):
            a = jnp.concatenate([amps[f, t, pl.ds(parity, HALF, stride=2), :] for t in range(2)], axis=1)
            squares = a * a
            sums = sums + (squares[:, :128] + squares[:, 128:]).reshape(16, 8, 128).sum(axis=0)
            high = a.astype(BF16)
            rest = a - high.astype(F32)
            middle = rest.astype(BF16)
            low = (rest - middle.astype(F32)).astype(BF16)
            parts.append(jnp.concatenate([high, middle, low], axis=1))
        both = jnp.concatenate(parts, axis=0)
        sorter = sort[...]
        sorted_amp[f] = jnp.dot(
            both, jnp.concatenate([sorter, sorter, sorter], axis=0), preferred_element_type=F32
        )
    early0[pl.ds(W, 8), :] = sums

    at_row = [pos[0, 0, 0, f] for f in range(FRAMES)]
    at_col = [pos[0, 0, 1, f] for f in range(FRAMES)]

    def gather(f, p, row):
        b = at_col[f]
        tiles = [ext[p, t, pl.ds(at_row[f] + row, STEP), :] for t in range(3)]
        turned = [pltpu.roll(t, lax.rem(128 - b, 128), 1) for t in tiles]
        keep = lane < 128 - b
        return jnp.concatenate(
            [jnp.where(keep, turned[0], turned[1]), jnp.where(keep, turned[1], turned[2])], axis=1
        )

    def scatter(f, p, row, value):
        b = at_col[f]
        behind = lane >= b
        v0, v1 = pltpu.roll(value[:, :128], b, 1), pltpu.roll(value[:, 128:], b, 1)
        at = pl.ds(LEAD + row, STEP)
        spread[f, p, 0, at, :] = jnp.where(behind, v0, zero)
        spread[f, p, 1, at, :] = jnp.where(behind, v1, v0)
        spread[f, p, 2, at, :] = jnp.where(behind, zero, v1)

    for row in range(0, W, STEP):
        here = pl.ds(row, STEP)
        pr, pi = probe[0, here, :], probe[1, here, :]
        for f in range(FRAMES):
            scatter(f, 2, row, pr * pr + pi * pi)

    def gather_canvas(planes):
        def some(i, _):
            row = pl.multiple_of(16 * i, 16)
            for p in planes:
                for t in range(3):
                    total = spread[0, p, t, pl.ds(LEAD - at_row[0] + row, 16), :]
                    for f in range(1, FRAMES):
                        total = total + spread[f, p, t, pl.ds(LEAD - at_row[f] + row, 16), :]
                    canvas[p, t, pl.ds(row, 16), :] = total
            return 0

        lax.fori_loop(0, SIDE // 16, some, 0)

    lane8 = lanes()
    first = lane8 < 32
    second = lane8 < 64
    zero8 = jnp.zeros((8, 128), F32)
    has_n, has_s = r > 0, r < rows - 1
    has_w, has_e = c > 0, c < cols - 1

    def strip(ref, at, q, target, keep):
        amount = (target - 32 * q) % 128
        block = ref[at]
        block = pltpu.roll(block, amount, 1) if amount else block
        return jnp.where(keep, block, zero8)

    def pack_edges(planes):
        for p in planes:
            for side, base in enumerate((0, MARGIN + W)):
                for q in range(4):
                    t = [pltpu.roll(canvas[p, i, pl.ds(base + 8 * q, 8), :], 96, 1) for i in range(3)]
                    bands[side, p, pl.ds(8 * q, 8), 0:128] = jnp.where(lane8 < 96, t[0], t[1])
                    bands[side, p, pl.ds(8 * q, 8), 128:256] = jnp.where(lane8 < 96, t[1], t[2])
            for j in range(10):
                left = [canvas[p, 0, pl.ds(32 * j + 8 * q, 8), :] for q in range(4)]
                right = [canvas[p, 2, pl.ds(32 * j + 8 * q, 8), :] for q in range(4)]
                strips[0, p, pl.ds(8 * j, 8), :] = pack(left, 0)
                strips[1, p, pl.ds(8 * j, 8), :] = pack(right, 96)

    def send_edges(planes):
        at = pl.ds(planes[0], len(planes))
        moves = (
            (bands.at[0, at], from_ns.at[1, at]),
            (bands.at[1, at], from_ns.at[0, at]),
            (strips.at[0, at, 8:72, :], from_we.at[1, at]),
            (strips.at[1, at, 8:72, :], from_we.at[0, at]),
            (strips.at[0, at, 0:8, :], from_corner.at[3, at]),
            (strips.at[1, at, 0:8, :], from_corner.at[2, at]),
            (strips.at[0, at, 72:80, :], from_corner.at[1, at]),
            (strips.at[1, at, 72:80, :], from_corner.at[0, at]),
        )
        for i in (4, 5, 6, 7, 0, 1, 2, 3):
            send(moves[i][0], moves[i][1], send_edge, recv_edge, around[i])

    gather_canvas((2,))
    pack_edges((2,))
    loads[3].wait()

    def put(p, row, centre, west, east):
        t0, t1 = pltpu.roll(centre[0], 32, 1), pltpu.roll(centre[1], 32, 1)
        ext[p, 0, pl.ds(row, 8), :] = jnp.where(first, west, t0)
        ext[p, 1, pl.ds(row, 8), :] = jnp.where(first, t0, t1)
        ext[p, 2, pl.ds(row, 8), :] = jnp.where(first, t1, jnp.where(second, east, zero8))

    arrive(room(2 * 2 * 64 * 128), recv_halo.at[1])
    for p in range(2):
        for j in range(8):
            for q in range(4):
                at = 32 * j + 8 * q
                block = obj[p, pl.ds(at, 8), :]
                west = strip(halo_we, (0, p, pl.ds(8 * j, 8)), q, 0, has_w)
                east = strip(halo_we, (1, p, pl.ds(8 * j, 8)), q, 32, has_e)
                put(p, MARGIN + at, (block[:, :128], block[:, 128:]), west, east)
    def halve(f, stage, side, rows_at, value):
        h, l = split(value)
        half[stage, side, 0, pl.ds(W * f + rows_at.start, rows_at.size), :] = h
        half[stage, side, 1, pl.ds(W * f + rows_at.start, rows_at.size), :] = l

    def first_step(some_rows):
        for row in some_rows:
            sums = [jnp.zeros((STEP, W), F32)] * 2
            for f in range(FRAMES):
                waves = []
                for i, base in enumerate((row, HALF + row)):
                    here = pl.ds(base, STEP)
                    wr, wi = gather(f, 0, base), gather(f, 1, base)
                    pr, pi = probe[0, here, :], probe[1, here, :]
                    win[f, 0, here, :] = wr
                    win[f, 1, here, :] = wi
                    sums[i] = sums[i] + (wr * wr + wi * wi)
                    waves.append((pr * wr - pi * wi, pr * wi + pi * wr))
                    wave[f, 0, here, :], wave[f, 1, here, :] = waves[-1]
                for part in range(2):
                    top, low = waves[0][part], waves[1][part]
                    where = pl.ds(HALF * part + row, STEP)
                    halve(f, 0, 0, where, top + low)
                    halve(f, 0, 1, where, top - low)
            for i, base in enumerate((row, HALF + row)):
                power2[pl.ds(base, STEP), :] = sums[i][:, :128]
                power2[pl.ds(W + base, STEP), :] = sums[i][:, 128:]

    first_step(range(MARGIN, HALF - MARGIN, STEP))
    arrive(room(2 * 2 * 32 * W + 4 * 2 * 8 * 128), recv_halo.at[0])
    for p in range(2):
        for k in range(4):
            for side, (keep_v, base) in enumerate(((has_n, 0), (has_s, MARGIN + W))):
                block = halo_ns[side, p, pl.ds(8 * k, 8), :]
                block = jnp.where(keep_v, block, jnp.zeros_like(block))
                west = strip(halo_corner, (2 * side, p, slice(0, 8)), k, 0, has_w & keep_v)
                east = strip(halo_corner, (2 * side + 1, p, slice(0, 8)), k, 32, has_e & keep_v)
                put(p, base + 8 * k, (block[:, :128], block[:, 128:]), west, east)

    send_edges((2,))
    first_step([*range(0, MARGIN, STEP), *range(HALF - MARGIN, HALF, STEP)])

    mine8 = pl.multiple_of(core * HALF, HALF)
    other8 = pl.multiple_of((1 - core) * HALF, HALF)
    for t in range(2):
        early0[pl.ds(HALF * t, HALF), :] = power2[pl.ds(W * t + other8, HALF), :]
    e0 = send(early0, early0_got, send_pair.at[0], recv_pair.at[0], pair)

    def left_dots(stage, flip):
        for f in range(FRAMES):
            here = pl.ds(W * f, W)
            for side in range(2):
                mid[stage, side, here, :] = triple(
                    (table[flip + side, 0], table[flip + side, 1]),
                    (half[stage, side, 0, here, :], half[stage, side, 1, here, :]),
                )

    def right_dots(stage, flip):
        for side in range(2):
            mid[stage, side] = triple(
                (half[stage, side, 0], half[stage, side, 1]),
                (table[flip + side, 0], table[flip + side, 1]),
            )

    left_dots(0, 0)
    for f in range(FRAMES):
        for parity in range(2):
            for row in range(0, HALF, STEP):
                zr = mid[0, parity, pl.ds(W * f + row, STEP), :]
                zi = mid[0, parity, pl.ds(W * f + HALF + row, STEP), :]
                here = pl.ds(HALF * parity + row, STEP)
                plus = jnp.concatenate([zr[:, :128] + zr[:, 128:], zi[:, :128] + zi[:, 128:]], axis=1)
                less = jnp.concatenate([zr[:, :128] - zr[:, 128:], zi[:, :128] - zi[:, 128:]], axis=1)
                halve(f, 1, 0, here, plus)
                halve(f, 1, 1, here, less)

    right_dots(1, 2)
    for f in range(FRAMES):
        for side in range(2):
            for row in range(0, W, STEP):
                here = pl.ds(row, STEP)
                amp = sorted_amp[f, here, 128 * side : 128 * side + 128]
                v = mid[1, side, pl.ds(W * f + row, STEP), :]
                zr, zi = v[:, :128], v[:, 128:]
                factor = amp * lax.rsqrt(zr * zr + zi * zi + smoothing)
                halve(f, 2, side, here, jnp.concatenate([zr * factor, zi * factor], axis=1))

    k = 4 * x + y
    e0.wait_recv()
    for i in range(16):
        for t in range(2):
            at = mine8 + 8 * i
            early1[i, pl.ds(8 * t, 8), :] = (
                power2[pl.ds(W * t + at, 8), :] + early0_got[pl.ds(HALF * t + 8 * i, 8), :]
            )
        early1[i, pl.ds(16, 8), :] = early0[pl.ds(W, 8), :] + early0_got[pl.ds(W, 8), :]
    early1_got[k] = early1[k]
    e1 = []
    for i, (x_, y_) in enumerate(on_plane):
        e1.append(send(early1.at[4 * x_ + y_], early1_got.at[k], send_e1.at[0], recv_e1.at[0], plane[i]))

    right_dots(2, 0)

    for f in range(FRAMES):
        for parity in range(2):
            for row in range(0, HALF, STEP):
                even, odd = (mid[2, i, pl.ds(W * f + HALF * parity + row, STEP), :] for i in range(2))
                plus, less = even + odd, even - odd
                for part in range(2):
                    cut = slice(128 * part, 128 * part + 128)
                    value = jnp.concatenate([plus[:, cut], less[:, cut]], axis=1)
                    halve(f, 3, parity, pl.ds(HALF * part + row, STEP), value)

    left_dots(3, 2)
    for row in range(0, HALF, STEP):
        parts = []
        for f in range(FRAMES):
            er, orr = (mid[3, i, pl.ds(W * f + row, STEP), :] for i in range(2))
            ei, oi = (mid[3, i, pl.ds(W * f + HALF + row, STEP), :] for i in range(2))
            parts.append(((er + orr, ei + oi), (er - orr, ei - oi)))
        for side, base in enumerate((row, HALF + row)):
            here = pl.ds(base, STEP)
            pr, pi = probe[0, here, :], probe[1, here, :]
            sums = [jnp.zeros((STEP, W), F32)] * 2
            for f in range(FRAMES):
                wr, wi = win[f, 0, here, :], win[f, 1, here, :]
                dr = parts[f][side][0] - wave[f, 0, here, :]
                di = parts[f][side][1] - wave[f, 1, here, :]
                scatter(f, 0, base, pr * dr + pi * di)
                scatter(f, 1, base, pr * di - pi * dr)
                sums = [sums[0] + (wr * dr + wi * di), sums[1] + (wr * di - wi * dr)]
            acc[0, here, :], acc[1, here, :] = sums

    mine = pl.ds(mine8, HALF)
    other = pl.ds(other8, HALF)
    c0 = [
        send(acc.at[p, other, :], got0.at[p], send_pair.at[1 + p], recv_pair.at[1 + p], pair) for p in range(2)
    ]

    gather_canvas((0, 1))

    c1 = []
    for p in range(2):
        c0[p].wait_recv()
        part0[p] = acc[p, mine, :] + got0[p]
        for i, (x_, y_) in enumerate(on_plane):
            src = part0.at[p, pl.ds(pl.multiple_of(8 * (4 * x_ + y_), 8), 8), :]
            c1.append(send(src, got1.at[p, i], send_m1.at[p], recv_m1.at[p], plane[i]))

    pack_edges((0, 1))
    arrive(early1_got.at[0:15], recv_e1.at[0])
    total = early1_got[0]
    for i in range(1, 16):
        total = total + early1_got[i]
    early2[z] = total
    e2 = [send(early2.at[z], early2.at[z], send_e2.at[0], recv_e2.at[0], column[i]) for i in range(7)]

    own = pl.ds(pl.multiple_of(8 * k, 8), 8)
    c2 = []
    for p in range(2):
        arrive(got1.at[p], recv_m1.at[p])
        total = part0[p, own, :]
        for i in range(15):
            total = total + got1[p, i]
        all2[p, z] = total
        for i in range(7):
            c2.append(
                send(all2.at[p, z], all2.at[p, z], send_m2.at[p], recv_m2.at[p], column[i])
            )

    send_edges((0, 1))

    arrive(early2.at[0:7], recv_e2.at[0])
    total = early2[0]
    for i in range(1, 8):
        total = total + early2[i]
    weight = 1.0 / (jnp.concatenate([total[0:8], total[8:16]], axis=1) + regular)
    target = jnp.sum(total[16:24]) * (1.0 / (FRAMES * rows * cols))

    block = pl.ds(pl.multiple_of(HALF * core + 8 * k, 8), 8)
    for p in range(2):
        arrive(all2.at[p, 0:7], recv_m2.at[p])
        total = all2[p, 0]
        for i in range(1, 8):
            total = total + all2[p, i]
        gathered[p, block, :] = probe[p, block, :] + total * weight
        here = gathered.at[p, block, :]
        for i in range(15):
            send(here, here, send_ag.at[p], recv_ag.at[4 * p + far[i]], plane[i])
        send(here, here, send_fw.at[p], recv_fw.at[p], pair)

    for p in range(2):
        for distance in range(4):
            batch = [i for i in range(15) if far[i] == distance]
            arrive(gathered.at[p, 0 : 8 * len(batch)], recv_ag.at[4 * p + distance])
            for i in batch:
                x_, y_ = behind_plane[i]
                here = gathered.at[p, pl.ds(pl.multiple_of(HALF * core + 8 * (4 * x_ + y_), 8), 8), :]
                send(here, here, send_fw.at[p], recv_fw.at[p], pair)
    arrive(room(3 * (2 * 32 * W + 2 * 64 * 128 + 4 * 8 * 128)), recv_edge)
    for j in range(8):
        for q in range(4):
            at = 32 * j + 8 * q
            totals = []
            for p in range(3):
                t = [pltpu.roll(canvas[p, i, pl.ds(MARGIN + at, 8), :], 96, 1) for i in range(3)]
                left = jnp.where(lane8 < 96, t[0], t[1])
                right = jnp.where(lane8 < 96, t[1], t[2])
                if j in (0, 7):
                    side = 0 if j == 0 else 1
                    keep_v = has_n if j == 0 else has_s
                    band = from_ns[side, p, pl.ds(8 * q, 8), :]
                    left = left + jnp.where(keep_v, band[:, :128], zero8)
                    right = right + jnp.where(keep_v, band[:, 128:], zero8)
                    west = strip(from_corner, (2 * side, p, slice(0, 8)), q, 0, has_w & keep_v)
                    east = strip(from_corner, (2 * side + 1, p, slice(0, 8)), q, 96, has_e & keep_v)
                    left = left + jnp.where(first, west, zero8)
                    right = right + jnp.where(lane8 >= 96, east, zero8)
                west = strip(from_we, (0, p, pl.ds(8 * j, 8)), q, 0, has_w)
                east = strip(from_we, (1, p, pl.ds(8 * j, 8)), q, 96, has_e)
                left = left + jnp.where(first, west, zero8)
                right = right + jnp.where(lane8 >= 96, east, zero8)
                totals.append((left, right))
            for s in range(2):
                scale = 1.0 / (totals[2][s] + regular)
                for p in range(2):
                    here = (p, pl.ds(at, 8), slice(128 * s, 128 * s + 128))
                    out_obj[here] = obj[here] + totals[p][s] * scale

    for copy in [e0] + c0:
        copy.wait_send()
    sent(room(2 * (2 * 32 * W + 2 * 64 * 128 + 4 * 8 * 128)), send_halo)
    sent(room(3 * (2 * 32 * W + 2 * 64 * 128 + 4 * 8 * 128)), send_edge)
    sent(early1.at[0:15], send_e1.at[0])
    sent(early2.at[0:7], send_e2.at[0])
    for p in range(2):
        sent(got1.at[p], send_m1.at[p])
        sent(all2.at[p, 0:7], send_m2.at[p])

    for p in range(2):
        arrive(gathered.at[p, other, :], recv_fw.at[p])
    power = jnp.zeros((8, W), F32)
    for p in range(2):
        g = gathered[p]
        power = power + (g * g).reshape(32, 8, W).sum(axis=0)
    scale = jnp.sqrt(jnp.full((8, W), target, F32) / (jnp.sum(power) + epsilon))
    for p in range(2):
        out_probe[p] = gathered[p] * jnp.concatenate([scale] * 32, axis=0)

    for p in range(2):
        sent(gathered.at[p, 0:120], send_ag.at[p])
        sent(gathered.at[p, mine, :], send_fw.at[p])


def write_kernel(obj, probe, out_obj, out_probe, sems):
    copies = [
        pltpu.make_async_copy(obj, out_obj, sems.at[0]),
        pltpu.make_async_copy(probe, out_probe, sems.at[1]),
    ]
    for copy in copies:
        copy.start()
    for copy in copies:
        copy.wait()


def vmem(*shape, dtype=F32):
    return pltpu.VMEM(shape, dtype)


def per_device(rows, cols, object_field, probe, amplitudes, positions):
    in_vmem = pl.BlockSpec(memory_space=pltpu.VMEM)
    in_hbm = pl.BlockSpec(memory_space=pltpu.HBM)
    dma = pltpu.SemaphoreType.DMA
    results = pl.pallas_call(
        functools.partial(kernel, rows, cols),
        out_shape=(jax.ShapeDtypeStruct((2, W, W), F32),) * 2,
        in_specs=[in_hbm] * 6,
        out_specs=(in_vmem,) * 2,
        scratch_shapes=[
            pltpu.SMEM((1, 1, 2, FRAMES), jnp.int32),
            vmem(2, W, W),
            vmem(2, W, W),
            vmem(FRAMES, 2, W, 128),
            vmem(4, 2, W, W, dtype=BF16),
            vmem(W, W, dtype=BF16),
            vmem(2, 2, 64, 128),
            vmem(2, 2, 32, W),
            vmem(2, 2, 64, 128),
            vmem(4, 2, 8, 128),
            vmem(2, 3, SIDE, 128),
            vmem(FRAMES, 3, 3, LEAD + W + LEAD, 128),
            vmem(FRAMES, 2, W, W),
            vmem(FRAMES, 2, W, W),
            vmem(FRAMES, W, W),
            vmem(4, 2, 2, FRAMES * W, W, dtype=BF16),
            vmem(4, 2, FRAMES * W, W),
            vmem(2, W, W),
            vmem(2 * W, 128),
            vmem(3, 3, SIDE, 128),
            vmem(2, 3, 80, 128),
            vmem(2, 3, 32, W),
            vmem(2, 3, 32, W),
            vmem(2, 3, 64, 128),
            vmem(4, 3, 8, 128),
            vmem(W + 8, 128),
            vmem(W + 8, 128),
            vmem(16, 24, 128),
            vmem(16, 24, 128),
            vmem(8, 24, 128),
            vmem(2, HALF, W),
            vmem(2, HALF, W),
            vmem(2, 15, 8, W),
            vmem(2, 8, 8, W),
            vmem(2, W, W),
            dma((5,)),
            dma,
            dma,
            dma((2,)),
            dma,
            dma,
            dma((3,)),
            dma((3,)),
            dma((1,)),
            dma((1,)),
            dma((1,)),
            dma((1,)),
            dma((2,)),
            dma((2,)),
            dma((2,)),
            dma((2,)),
            dma((2,)),
            dma((8,)),
            dma((2,)),
            dma((2,)),
        ],
        compiler_params=pltpu.CompilerParams(
            collective_id=0, has_side_effects=True, vmem_limit_bytes=48 * 2**20
        ),
        name="ptycho",
    )(
        *(
            pltpu.with_memory_space_constraint(a, pltpu.HBM)
            for a in (
                jnp.swapaxes(positions, 2, 3),
                object_field,
                probe,
                amplitudes,
                jnp.asarray(dft_tables()),
                jnp.asarray(sort_table()),
            )
        ),
    )
    return pl.pallas_call(
        write_kernel,
        out_shape=(jax.ShapeDtypeStruct((2, W, W), F32),) * 2,
        in_specs=[in_vmem] * 2,
        out_specs=(in_hbm,) * 2,
        scratch_shapes=[dma((2,))],
        compiler_params=pltpu.CompilerParams(vmem_limit_bytes=2**20),
        name="write",
    )(*results)


def solution(mesh):
    return jax.shard_map(
        functools.partial(per_device, mesh.shape["row"], mesh.shape["col"]),
        mesh=mesh,
        in_specs=(
            P(None, "row", "col"),
            P(),
            P("row", "col", None, None, None),
            P("row", "col", None, None),
        ),
        out_specs=(P(None, "row", "col"), P()),
        check_vma=False,
    )
```
